256 devices in a mesh: expert: 4 (over x_lo, core), node: 64 (over y, z, x_hi).
Axes of the slice: x: 4 (x_hi: 2, x_lo: 2; x = x_hi * 2 + x_lo), y: 4, z: 8, core: 2. Of those that a mesh axis runs over, the one named last changes fastest.
Arguments:
- tokens: bfloat16 [2, 65536, 1024], P(None, ('expert', 'node')), may hold values from -6 to 6
- routing: int32 [2, 65536], P(None, ('expert', 'node')), may hold values from 0 to 3, as said below
- out_grad: bfloat16 [2, 65536, 512], P(None, ('expert', 'node')), may hold values from -6 to 6
- weights: float32 [64, 4, 1024, 512], P('node', 'expert'), may hold values from -5 to 5
- momentum: float32 [64, 4, 1024, 512], P('node', 'expert'), may hold values from -8 to 8
Outputs:
- new_weights: float32 [64, 4, 1024, 512], P('node', 'expert')
- new_momentum: float32 [64, 4, 1024, 512], P('node', 'expert')
- in_grad: bfloat16 [2, 65536, 1024], P(None, ('expert', 'node'))
The draws below stay inside these ranges and needn't reach their ends.
Inputs may be any that keep to these rules, and one draw needn't show every extreme that they name: `routing`: within each block of 256 rows of one round (the rows of one device), no expert is named more than 128 times; in every round each node has one expert that is named exactly 128 times in each of that node's blocks.
All inputs are finite; a program needn't handle non-finite values.
Results may differ from the reference program's by a relative error of at most 0.0065.
Values may be sent and summed in bfloat16 or wider, within the bound.
A program may use at most 64 MiB of HBM per device.

```python
import math
import jax
import jax.numpy as jnp
from jax import lax

D = 1024
H = 512
TOK_DEV = 256
ROUNDS = 2
NS_STEPS = 3
EXPERTS = 4
CAP = 128
NODES = 64
TOKENS = 65536
N_EXPERT = 4


def draw_routing(key, part):
    blocks = TOKENS // TOK_DEV
    full_key, cut_key, order_key = jax.random.split(key, 3)
    full_pick = jax.random.randint(full_key, (ROUNDS, 1, NODES), 0, EXPERTS)
    full_pick = jnp.broadcast_to(full_pick, (ROUNDS, blocks // NODES, NODES)).reshape(ROUNDS, blocks, 1)
    spare_rows = TOK_DEV - CAP
    cut_points = jnp.sort(jax.random.randint(cut_key, (ROUNDS, blocks, EXPERTS - 2), 0, spare_rows + 1), axis=-1)
    upper_edges = jnp.concatenate([cut_points, jnp.full((ROUNDS, blocks, 1), spare_rows, jnp.int32)], axis=-1)
    places = jnp.arange(TOK_DEV, dtype=jnp.int32)
    beyond = places - CAP
    passed = jnp.sum((beyond[None, None, :, None] >= upper_edges[:, :, None, :]).astype(jnp.int32), axis=-1)
    others = (full_pick + 1 + passed) % EXPERTS
    labels = jnp.where(places[None, None, :] < CAP, full_pick, others)
    scores = jax.random.randint(order_key, (ROUNDS, blocks, TOK_DEV), 0, 1048576) * TOK_DEV + places[None, None, :]
    shuffle = jnp.argsort(scores, axis=-1)
    labels = jnp.take_along_axis(labels, shuffle, axis=-1)
    return labels.reshape(ROUNDS, TOKENS).astype(jnp.int32)


def draw_momentum(key, part):
    base_key = jax.random.fold_in(key, 0)
    values = jax.random.normal(base_key, (NODES, EXPERTS, D, H), jnp.float32)
    return jnp.clip(values, -8.0, 8.0)


def level_of(own_key, dims, cuts, low, top_value):
    def one(position, shards_of):
        heights = jax.random.uniform(jax.random.fold_in(jax.random.fold_in(own_key, 6), position), (shards_of,), jnp.float32, low / len(cuts), top_value / len(cuts))
        return jnp.repeat(jnp.exp(heights), dims[position] // shards_of).reshape((-1,) + (1,) * (len(dims) - position - 1))

    level = one(*cuts[0])
    for cut in cuts[1:]:
        level = level * one(*cut)
    return level


def scatter_about(key, shape, width, reach, pieces=(), kind=jnp.bfloat16):
    loudness = level_of(key, shape, pieces, -0.22, 0.18) if pieces else 1.0
    drawn = jax.random.normal(key, shape, jnp.float32) * width * loudness
    return jnp.minimum(jnp.maximum(drawn, -reach), reach).astype(kind)


def setup_inputs(seed: int = 0) -> dict:
    key_of = jax.random.split(jax.random.key(seed), 6)
    return {
        "tokens": scatter_about(key_of[0], (ROUNDS, TOKENS, D), 1.0, 6.0, ((1, 256),)),
        "routing": draw_routing(jax.random.fold_in(key_of[5], 71), 0),
        "out_grad": scatter_about(key_of[2], (ROUNDS, TOKENS, H), 1.0, 6.0, ((1, 256),)),
        "weights": scatter_about(key_of[3], (NODES, EXPERTS, D, H), 1.0, 5.0, ((0, 64), (1, 4)), jnp.float32),
        "momentum": draw_momentum(jax.random.fold_in(key_of[5], 71), 0),
    }


def rounded(value):
    return lax.optimization_barrier(value.astype(jnp.bfloat16))

def per_node(item):
    node_tokens, node_grads, node_routes, node_weight, node_moment = item
    factor = 1.0 / math.sqrt(D)
    step_size = 0.1 * math.sqrt(D)
    labels = jnp.arange(EXPERTS, dtype=jnp.int32)
    onehot = (node_routes[:, :, None] == labels[None, None, :]).astype(jnp.int32)
    slot_rank = lax.optimization_barrier(jnp.sum(onehot * (jnp.cumsum(onehot, axis=1) - 1), axis=-1))
    sources = jnp.arange(N_EXPERT, dtype=jnp.int32)[:, None]
    target = (node_routes * (N_EXPERT * CAP) + sources * CAP + slot_rank).reshape(-1).astype(jnp.int32)
    row_buffer = jnp.zeros((EXPERTS * N_EXPERT * CAP, D), jnp.bfloat16)
    row_buffer = row_buffer.at[target].set(node_tokens.reshape(-1, D)).reshape(EXPERTS, N_EXPERT * CAP, D)
    grad_buffer = jnp.zeros((EXPERTS * N_EXPERT * CAP, H), jnp.bfloat16)
    grad_buffer = grad_buffer.at[target].set(node_grads.reshape(-1, H)).reshape(EXPERTS, N_EXPERT * CAP, H)
    shaped = rounded(node_weight).astype(jnp.float32)
    preact = jnp.einsum('erd,edh->erh', row_buffer.astype(jnp.float32), shaped) * factor
    slopes = rounded(grad_buffer.astype(jnp.float32) * 2.0 * jnp.maximum(preact, 0.0))
    slope_wide = slopes.astype(jnp.float32)
    backward = rounded(jnp.einsum('erh,edh->erd', slope_wide, shaped) * factor)
    grad_w = jnp.einsum('erd,erh->edh', row_buffer.astype(jnp.float32), slope_wide) * factor
    row_grads = backward.reshape(-1, D)[target].reshape(N_EXPERT, TOK_DEV, D)
    moment = 0.9 * node_moment + grad_w
    frob_norm = jnp.sqrt(lax.optimization_barrier(jnp.sum(moment * moment, axis=(1, 2), keepdims=True)))
    orthog = rounded(moment / (frob_norm + 1e-07))
    for sweep in range(NS_STEPS):
        orth_wide = orthog.astype(jnp.float32)
        gram_matrix = rounded(jnp.einsum('edh,edk->ehk', orth_wide, orth_wide))
        gram_wide = gram_matrix.astype(jnp.float32)
        square = jnp.einsum('ehk,ekj->ehj', gram_wide, gram_wide)
        polynom = rounded(-4.775 * gram_wide + 2.0315 * square)
        orthog = rounded(3.4445 * orth_wide + jnp.einsum('edh,ehk->edk', orth_wide, polynom.astype(jnp.float32)))
    stepped = node_weight - step_size * orthog.astype(jnp.float32)
    return (stepped, moment, row_grads)

def reference(tokens, routing, out_grad, weights, momentum):
    weight = weights
    moment = momentum
    in_grads = []
    for round_index in range(ROUNDS):
        node_tokens = tokens[round_index].reshape(N_EXPERT, NODES, TOK_DEV, D).transpose(1, 0, 2, 3)
        node_grads = out_grad[round_index].reshape(N_EXPERT, NODES, TOK_DEV, H).transpose(1, 0, 2, 3)
        node_routes = routing[round_index].reshape(N_EXPERT, NODES, TOK_DEV).transpose(1, 0, 2)
        stepped, moment, row_grads = lax.map(per_node, (node_tokens, node_grads, node_routes, weight, moment))
        in_grads.append(row_grads.transpose(1, 0, 2, 3).reshape(TOKENS, D))
        shared = rounded(stepped).astype(jnp.float32)
        neighbours = jnp.roll(shared, 1, axis=0) + jnp.roll(shared, -1, axis=0)
        neighbours = neighbours + jnp.roll(shared, 2, axis=0) + jnp.roll(shared, -2, axis=0)
        weight = 0.4 * stepped + 0.15 * neighbours
    return (weight, moment, jnp.stack(in_grads))
```

```python
import math

import jax
import jax.numpy as jnp
from jax import lax
from jax.sharding import PartitionSpec as P

ROUNDS = 2
NS_STEPS = 3


def dispatch_table(route, experts_all, capacity):
    rows = route.shape[0]
    labels = jnp.arange(experts_all, dtype=jnp.int32)
    onehot = (route[:, None] == labels[None, :])
    places = jnp.arange(rows, dtype=jnp.int32)
    earlier = (places[:, None] > places[None, :]).astype(jnp.bfloat16)
    ranks = jnp.dot(earlier, onehot.astype(jnp.bfloat16), preferred_element_type=jnp.float32)
    slot_rank = jnp.sum(jnp.where(onehot, ranks, 0.0), axis=1).astype(jnp.int32)
    target = route * capacity + slot_rank
    slot_ids = jnp.arange(experts_all * capacity, dtype=jnp.int32)
    return (slot_ids[:, None] == target[None, :]).astype(jnp.bfloat16)


def orthogonalize(moment):
    frob_norm = jnp.sqrt(jnp.sum(moment * moment))
    orthog = (moment / (frob_norm + 1e-07)).astype(jnp.bfloat16)
    for sweep in range(NS_STEPS):
        gram_matrix = lax.dot_general(
            orthog, orthog, (((0,), (0,)), ((), ())), preferred_element_type=jnp.float32
        ).astype(jnp.bfloat16)
        square = jnp.dot(gram_matrix, gram_matrix, preferred_element_type=jnp.float32)
        polynom = (-4.775 * gram_matrix.astype(jnp.float32) + 2.0315 * square).astype(jnp.bfloat16)
        orthog = (
            3.4445 * orthog.astype(jnp.float32)
            + jnp.dot(orthog, polynom, preferred_element_type=jnp.float32)
        ).astype(jnp.bfloat16)
    return orthog


def neighbour_sum(shared):
    nodes = lax.axis_size("node")
    below = lax.ppermute(shared, "node", [((i - 2) % nodes, i) for i in range(nodes)])
    above = lax.ppermute(shared, "node", [((i + 2) % nodes, i) for i in range(nodes)])
    even = lax.axis_index("node") % 2 == 0
    beside = jnp.where(even, above, below)
    pair = (shared.astype(jnp.float32) + beside.astype(jnp.float32)).astype(jnp.bfloat16)
    across = lax.ppermute(pair, "node", [(i ^ 1, i) for i in range(nodes)])
    return below.astype(jnp.float32) + above.astype(jnp.float32) + across.astype(jnp.float32)


def on_device(tokens, routing, out_grad, weights, momentum):
    row_count = tokens.shape[1]
    model_width = tokens.shape[2]
    hidden_width = out_grad.shape[2]
    capacity = row_count // 2
    experts_all = weights.shape[1] * lax.axis_size("expert")
    factor = 1.0 / math.sqrt(model_width)
    step_size = 0.1 * math.sqrt(model_width)
    weight = weights[0, 0]
    moment = momentum[0, 0]
    tables = []
    received = []
    for round_index in range(ROUNDS):
        dispatch = dispatch_table(routing[round_index], experts_all, capacity)
        tables.append(dispatch)
        rows = jnp.concatenate([tokens[round_index], out_grad[round_index]], axis=1)
        sent = jnp.dot(dispatch, rows, preferred_element_type=jnp.float32)
        sent = sent.astype(jnp.bfloat16).reshape(experts_all, capacity, -1)
        received.append(lax.all_to_all(sent, "expert", split_axis=0, concat_axis=0, tiled=True))
    in_grads = []
    for round_index in range(ROUNDS):
        got = received[round_index].reshape(-1, model_width + hidden_width)
        got_rows, got_grads = got[:, :model_width], got[:, model_width:]
        shaped = weight.astype(jnp.bfloat16)
        preact = jnp.dot(got_rows, shaped, preferred_element_type=jnp.float32) * factor
        slopes = (got_grads.astype(jnp.float32) * 2.0 * jnp.maximum(preact, 0.0)).astype(
            jnp.bfloat16
        )
        backward = (
            lax.dot_general(
                slopes, shaped, (((1,), (1,)), ((), ())), preferred_element_type=jnp.float32
            )
            * factor
        )
        backward = backward.astype(jnp.bfloat16).reshape(-1, capacity, model_width)
        grad_w = (
            lax.dot_general(
                got_rows, slopes, (((0,), (0,)), ((), ())), preferred_element_type=jnp.float32
            )
            * factor
        )
        returned = lax.all_to_all(
            backward, "expert", split_axis=0, concat_axis=0, tiled=True
        ).reshape(-1, model_width)
        in_grads.append(
            lax.dot_general(
                tables[round_index],
                returned,
                (((0,), (0,)), ((), ())),
                preferred_element_type=jnp.float32,
            ).astype(jnp.bfloat16)
        )
        moment = 0.9 * moment + grad_w
        orthog = orthogonalize(moment)
        stepped = weight - step_size * orthog.astype(jnp.float32)
        weight = 0.4 * stepped + 0.15 * neighbour_sum(stepped.astype(jnp.bfloat16))
    return (weight[None, None], moment[None, None], jnp.stack(in_grads))


def solution(mesh):
    return jax.shard_map(
        on_device,
        mesh=mesh,
        in_specs=(
            P(None, ("expert", "node"), None),
            P(None, ("expert", "node")),
            P(None, ("expert", "node"), None),
            P("node", "expert", None, None),
            P("node", "expert", None, None),
        ),
        out_specs=(
            P("node", "expert", None, None),
            P("node", "expert", None, None),
            P(None, ("expert", "node"), None),
        ),
        check_vma=False,
    )
```

```python
import functools
import math

import jax
import jax.numpy as jnp
from jax import lax
from jax.experimental import pallas as pl
from jax.experimental.pallas import tpu as pltpu
from jax.sharding import PartitionSpec as P

ROUNDS = 2
NS_STEPS = 3
CHUNKS = 4
MESH = pl.DeviceIdType.MESH
F32 = jnp.float32
BF16 = jnp.bfloat16


def dot(a, b, ca=1, cb=0):
    return lax.dot_general(a, b, (((ca,), (cb,)), ((), ())), preferred_element_type=F32)


def kernel(
    nodes, experts,
    tok_hbm, route_ref, og_hbm, w_hbm, m_hbm,
    w_out, m_out, ig_out,
    tok, og, weight, moment, wide, table, sent, got, slope, orthog, gram, poly,
    back, ret, ig, shared, beside, pair, across,
    in_sem, out_sem, w_sem, d_send, d_recv, r_send, r_recv, z_send, z_recv, x_send, x_recv,
):
    expert = lax.axis_index("expert")
    node = lax.axis_index("node")
    rows, width = tok.shape[1], tok.shape[2]
    hidden = og.shape[2]
    cap = rows // 2
    tile = width // CHUNKS
    factor = 1.0 / math.sqrt(width)
    step_size = 0.1 * math.sqrt(width)

    chip, core = expert // 2, expert % 2
    mates = (
        expert,
        2 * chip + (1 - core),
        2 * (1 - chip) + core,
        2 * (1 - chip) + (1 - core),
    )
    odd = node % 2
    up = (node + 2) % nodes
    down = (node + nodes - 2) % nodes
    facing = node + 1 - 2 * odd

    loads = []
    for r in range(ROUNDS):
        loads.append(pltpu.make_async_copy(tok_hbm.at[r], tok.at[r], in_sem.at[2 * r]))
        loads.append(pltpu.make_async_copy(og_hbm.at[r], og.at[r], in_sem.at[2 * r + 1]))
    load_w = pltpu.make_async_copy(w_hbm.at[0, 0], weight, in_sem.at[4])
    load_m = pltpu.make_async_copy(m_hbm.at[0, 0], moment, in_sem.at[5])
    for copy in (loads[0], loads[1], load_w, load_m, loads[2], loads[3]):
        copy.start()

    barrier = pltpu.get_barrier_semaphore()
    for mate in mates[1:]:
        pl.semaphore_signal(barrier, inc=1, device_id=(mate, node), device_id_type=MESH)
    for other in (up, down, facing):
        pl.semaphore_signal(barrier, inc=1, device_id=(expert, other), device_id_type=MESH)

    def block(index):
        return pl.ds(pl.multiple_of(index * cap, cap), cap)

    def fixed(index):
        return pl.ds(index * cap, cap)

    def strip(index):
        return pl.ds(pl.multiple_of(index * tile, tile), tile)

    def dispatch(r):
        route = route_ref[r : r + 1, :]
        mask = lax.broadcasted_iota(jnp.int32, (16, rows), 0) == route
        first = lax.broadcasted_iota(jnp.int32, (rows, rows), 0)
        second = lax.broadcasted_iota(jnp.int32, (rows, rows), 1)
        earlier = jnp.where(first < second, 1.0, 0.0).astype(BF16)
        ranks = dot(jnp.where(mask, 1.0, 0.0).astype(BF16), earlier)
        rank = jnp.sum(jnp.where(mask, ranks, 0.0), axis=0, keepdims=True)
        target = route.astype(F32) * float(cap) + rank
        for e in range(experts):
            slots = (lax.broadcasted_iota(jnp.int32, (cap, rows), 0) + e * cap).astype(F32)
            picks = jnp.where(slots == target, 1.0, 0.0).astype(BF16)
            table[r, fixed(e), :] = picks
            sent[r, fixed(e), :width] = dot(picks, tok[r]).astype(BF16)
            sent[r, fixed(e), width:] = dot(picks, og[r]).astype(BF16)

    def dispatch_copy(r, k):
        return pltpu.make_async_remote_copy(
            src_ref=sent.at[r, block(mates[k])],
            dst_ref=got.at[r, fixed(k)],
            send_sem=d_send.at[r, k],
            recv_sem=d_recv.at[r, k],
            device_id=(mates[k], node),
            device_id_type=MESH,
        )

    def return_copy(r, k):
        return pltpu.make_async_remote_copy(
            src_ref=back.at[r, fixed(k)],
            dst_ref=ret.at[r, block(expert)],
            send_sem=r_send.at[r, k],
            recv_sem=r_recv.at[r, k],
            device_id=(mates[k], node),
            device_id_type=MESH,
        )

    def z_copy(r, way, j):
        return pltpu.make_async_remote_copy(
            src_ref=shared.at[r, strip(j)],
            dst_ref=beside.at[r, way, strip(j)],
            send_sem=z_send.at[r, way, j],
            recv_sem=z_recv.at[r, way, j],
            device_id=(expert, down if way else up),
            device_id_type=MESH,
        )

    def x_copy(r, j):
        return pltpu.make_async_remote_copy(
            src_ref=pair.at[r, strip(j)],
            dst_ref=across.at[r, strip(j)],
            send_sem=x_send.at[r, j],
            recv_sem=x_recv.at[r, j],
            device_id=(expert, facing),
            device_id_type=MESH,
        )

    def start_dispatch(r):
        for k in (2, 3, 1):
            dispatch_copy(r, k).start()
        got[r, fixed(0), :] = sent[r, block(expert), :]

    def start_return(r):
        for k in (2, 3, 1):
            return_copy(r, k).start()
        ret[r, block(expert), :] = back[r, fixed(0), :]

    def slopes(r, half):
        part = pl.ds(half * rows, rows)
        pre = dot(got[r, part, :width], wide[...]) * factor
        grads = got[r, part, width:].astype(F32)
        slope[part, :] = (grads * 2.0 * jnp.maximum(pre, 0.0)).astype(BF16)

    def update_moment(r):
        def body(j, total):
            columns = pl.ds(pl.multiple_of(j * tile, tile), tile)
            grad = dot(got[r, :, columns], slope[...], 0, 0) * factor
            new = 0.9 * moment[strip(j), :] + grad
            moment[strip(j), :] = new
            return total + jnp.sum(new * new, axis=0, keepdims=True)

        total = lax.fori_loop(0, CHUNKS, body, jnp.zeros((1, hidden), F32))
        norm = jnp.sqrt(jnp.sum(total, axis=1, keepdims=True))
        scale = 1.0 / (norm + 1e-07)

        def scaled(j, carry):
            orthog[strip(j), :] = (moment[strip(j), :] * scale).astype(BF16)
            return carry

        lax.fori_loop(0, CHUNKS, scaled, 0)

    def polynomial():
        part = hidden // 2
        for i in range(2):
            columns = pl.ds(i * part, part)
            gram[columns, :] = dot(orthog[:, columns], orthog[...], 0, 0).astype(BF16)
        for i in range(2):
            columns = pl.ds(i * part, part)
            own = gram[columns, :]
            square = dot(own, gram[...])
            poly[columns, :] = (-4.775 * own.astype(F32) + 2.0315 * square).astype(BF16)

    def applied(j):
        own = orthog[strip(j), :]
        return (3.4445 * own.astype(F32) + dot(own, poly[...])).astype(BF16)

    def orthogonalize_and_share(r):
        def sweep(i, carry):
            polynomial()

            def body(j, inner):
                orthog[strip(j), :] = applied(j)
                return inner

            return lax.fori_loop(0, CHUNKS, body, carry)

        lax.fori_loop(0, NS_STEPS - 1, sweep, 0)
        polynomial()

        def last(j, carry):
            stepped = weight[strip(j), :] - step_size * applied(j).astype(F32)
            weight[strip(j), :] = stepped
            shared[r, strip(j), :] = stepped.astype(BF16)
            z_copy(r, 0, j).start()
            z_copy(r, 1, j).start()
            return carry

        lax.fori_loop(0, CHUNKS, last, 0)

    def backward(r):
        for half in range(2):
            part = pl.ds(half * rows, rows)

            def body(j, carry, part=part):
                columns = pl.ds(pl.multiple_of(j * tile, tile), tile)
                grad = dot(slope[part, :], wide[strip(j), :], 1, 1) * factor
                back[r, part, columns] = grad.astype(BF16)
                return carry

            lax.fori_loop(0, CHUNKS, body, 0)

    def unsort(r):
        for k in (1, 2, 3):
            return_copy(r, k).wait_recv()

        def body(j, carry):
            columns = pl.ds(pl.multiple_of(j * tile, tile), tile)
            ig[r, :, columns] = dot(table[r], ret[r, :, columns], 0, 0).astype(BF16)
            return carry

        lax.fori_loop(0, CHUNKS, body, 0)
        pltpu.make_async_copy(ig.at[r], ig_out.at[r], out_sem.at[r]).start()

    def pass_across(r):
        def body(j, carry):
            z_copy(r, 0, j).wait_recv()
            z_copy(r, 1, j).wait_recv()
            own = shared[r, strip(j), :].astype(F32)
            pair[r, strip(j), :] = (own + beside[r, 1 - odd, strip(j), :].astype(F32)).astype(BF16)
            x_copy(r, j).start()
            return carry

        lax.fori_loop(0, CHUNKS, body, 0)

    def averaged(r, j):
        x_copy(r, j).wait_recv()
        neighbours = beside[r, 0, strip(j), :].astype(F32) + beside[r, 1, strip(j), :].astype(F32)
        neighbours = neighbours + across[r, strip(j), :].astype(F32)
        new = 0.4 * weight[strip(j), :] + 0.15 * neighbours
        weight[strip(j), :] = new
        return new

    loads[0].wait()
    loads[1].wait()
    dispatch(0)
    pl.semaphore_wait(barrier, 6)
    start_dispatch(0)
    loads[2].wait()
    loads[3].wait()
    dispatch(1)
    load_w.wait()

    def narrow(j, carry):
        wide[strip(j), :] = weight[strip(j), :].astype(BF16)
        return carry

    lax.fori_loop(0, CHUNKS, narrow, 0)
    load_m.wait()
    dispatch_copy(0, 1).wait_recv()
    slopes(0, 0)
    dispatch_copy(0, 2).wait_recv()
    dispatch_copy(0, 3).wait_recv()
    start_dispatch(1)
    slopes(0, 1)
    update_moment(0)
    orthogonalize_and_share(0)
    backward(0)
    pass_across(0)

    def mixed(j, carry):
        wide[strip(j), :] = averaged(0, j).astype(BF16)
        return carry

    lax.fori_loop(0, CHUNKS, mixed, 0)

    start_return(0)
    for k in (1, 2, 3):
        dispatch_copy(1, k).wait_recv()
    slopes(1, 0)
    slopes(1, 1)
    update_moment(1)
    give_m = pltpu.make_async_copy(moment, m_out.at[0, 0], out_sem.at[2])
    give_m.start()
    orthogonalize_and_share(1)
    backward(1)
    start_return(1)
    pass_across(1)
    unsort(0)

    def finished(j, carry):
        averaged(1, j)
        pltpu.make_async_copy(weight.at[strip(j)], w_out.at[0, 0, strip(j)], w_sem.at[j]).start()
        return carry

    lax.fori_loop(0, CHUNKS, finished, 0)
    unsort(1)

    for r in range(ROUNDS):
        for k in (1, 2, 3):
            dispatch_copy(r, k).wait_send()
            return_copy(r, k).wait_send()

        def sent_all(j, carry, r=r):
            z_copy(r, 0, j).wait_send()
            z_copy(r, 1, j).wait_send()
            x_copy(r, j).wait_send()
            return carry

        lax.fori_loop(0, CHUNKS, sent_all, 0)
        pltpu.make_async_copy(ig.at[r], ig_out.at[r], out_sem.at[r]).wait()
    give_m.wait()

    def given(j, carry):
        pltpu.make_async_copy(weight.at[strip(j)], w_out.at[0, 0, strip(j)], w_sem.at[j]).wait()
        return carry

    lax.fori_loop(0, CHUNKS, given, 0)


def on_device(tokens, routing, out_grad, weights, momentum):
    rounds, rows, width = tokens.shape
    hidden = out_grad.shape[2]
    experts = weights.shape[1] * lax.axis_size("expert")
    nodes = lax.axis_size("node")
    slots = experts * (rows // 2)
    anywhere = pl.BlockSpec(memory_space=pl.ANY)
    dma = pltpu.SemaphoreType.DMA
    return pl.pallas_call(
        functools.partial(kernel, nodes, experts),
        name="muon_rounds",
        out_shape=(
            jax.ShapeDtypeStruct(weights.shape, F32),
            jax.ShapeDtypeStruct(momentum.shape, F32),
            jax.ShapeDtypeStruct(tokens.shape, BF16),
        ),
        in_specs=[anywhere, pl.BlockSpec(memory_space=pltpu.VMEM), anywhere, anywhere, anywhere],
        out_specs=(anywhere, anywhere, anywhere),
        scratch_shapes=[
            pltpu.VMEM((rounds, rows, width), BF16),
            pltpu.VMEM((rounds, rows, hidden), BF16),
            pltpu.VMEM((width, hidden), F32),
            pltpu.VMEM((width, hidden), F32),
            pltpu.VMEM((width, hidden), BF16),
            pltpu.VMEM((rounds, slots, rows), BF16),
            pltpu.VMEM((rounds, slots, width + hidden), BF16),
            pltpu.VMEM((rounds, slots, width + hidden), BF16),
            pltpu.VMEM((slots, hidden), BF16),
            pltpu.VMEM((width, hidden), BF16),
            pltpu.VMEM((hidden, hidden), BF16),
            pltpu.VMEM((hidden, hidden), BF16),
            pltpu.VMEM((rounds, slots, width), BF16),
            pltpu.VMEM((rounds, slots, width), BF16),
            pltpu.VMEM((rounds, rows, width), BF16),
            pltpu.VMEM((rounds, width, hidden), BF16),
            pltpu.VMEM((rounds, 2, width, hidden), BF16),
            pltpu.VMEM((rounds, width, hidden), BF16),
            pltpu.VMEM((rounds, width, hidden), BF16),
            dma((6,)),
            dma((3,)),
            dma((CHUNKS,)),
            dma((rounds, 4)),
            dma((rounds, 4)),
            dma((rounds, 4)),
            dma((rounds, 4)),
            dma((rounds, 2, CHUNKS)),
            dma((rounds, 2, CHUNKS)),
            dma((rounds, CHUNKS)),
            dma((rounds, CHUNKS)),
        ],
        compiler_params=pltpu.CompilerParams(
            collective_id=0, has_side_effects=True, vmem_limit_bytes=56 << 20
        ),
    )(tokens, routing, out_grad, weights, momentum)


def solution(mesh):
    return jax.shard_map(
        on_device,
        mesh=mesh,
        in_specs=(
            P(None, ("expert", "node"), None),
            P(None, ("expert", "node")),
            P(None, ("expert", "node"), None),
            P("node", "expert", None, None),
            P("node", "expert", None, None),
        ),
        out_specs=(
            P("node", "expert", None, None),
            P("node", "expert", None, None),
            P(None, ("expert", "node"), None),
        ),
        check_vma=False,
    )
```

```python
import functools
import math

import jax
import jax.numpy as jnp
from jax import lax
from jax.experimental import pallas as pl
from jax.experimental.pallas import tpu as pltpu
from jax.sharding import PartitionSpec as P

ROUNDS = 2
NS_STEPS = 3
CHUNKS = 4
PIECES = 8
MESH = pl.DeviceIdType.MESH
F32 = jnp.float32
BF16 = jnp.bfloat16


def dot(a, b, ca=1, cb=0):
    return lax.dot_general(a, b, (((ca,), (cb,)), ((), ())), preferred_element_type=F32)


def kernel(
    nodes,
    tok_hbm, route_hbm, og_hbm, w_hbm, m_hbm,
    weight, moment, ig,
    route_ref, tok, og, wide, table, sent, got, slope, orthog, gram, poly,
    back, ret, shared, beside, pair, across,
    in_sem, d_send, d_recv, r_send, r_recv, z_send, z_recv, x_send, x_recv,
):
    expert = lax.axis_index("expert")
    node = lax.axis_index("node")
    rows, width = tok.shape[1], tok.shape[2]
    hidden = og.shape[2]
    cap = rows // 2
    tile = width // CHUNKS
    piece = width // PIECES
    factor = 1.0 / math.sqrt(width)
    step_size = 0.1 * math.sqrt(width)

    chip, core = expert // 2, expert % 2
    mates = (
        expert,
        2 * chip + (1 - core),
        2 * (1 - chip) + core,
        2 * (1 - chip) + (1 - core),
    )
    odd = node % 2
    up = (node + 2) % nodes
    down = (node + nodes - 2) % nodes
    facing = node + 1 - 2 * odd

    loads = []
    for r in range(ROUNDS):
        loads.append(pltpu.make_async_copy(tok_hbm.at[r], tok.at[r], in_sem.at[2 * r]))
        loads.append(pltpu.make_async_copy(og_hbm.at[r], og.at[r], in_sem.at[2 * r + 1]))
    load_w = pltpu.make_async_copy(w_hbm.at[0, 0], weight, in_sem.at[4])
    load_route = pltpu.make_async_copy(route_hbm, route_ref, in_sem.at[6])
    load_m = pltpu.make_async_copy(m_hbm.at[0, 0], moment, in_sem.at[5])
    for copy in (load_route, *loads[:2]):
        copy.start()

    barrier = pltpu.get_barrier_semaphore()
    for mate in mates[1:]:
        pl.semaphore_signal(barrier, inc=1, device_id=(mate, node), device_id_type=MESH)
    for other in (up, down, facing):
        pl.semaphore_signal(barrier, inc=1, device_id=(expert, other), device_id_type=MESH)

    def fixed(index):
        return pl.ds(index * cap, cap)

    def strip(index):
        return pl.ds(pl.multiple_of(index * tile, tile), tile)

    def bit(index):
        return pl.ds(pl.multiple_of(index * piece, piece), piece)

    def targets(r):
        route = route_ref[r : r + 1, :]
        mask = lax.broadcasted_iota(jnp.int32, (16, rows), 0) == route
        first = lax.broadcasted_iota(jnp.int32, (rows, rows), 0)
        second = lax.broadcasted_iota(jnp.int32, (rows, rows), 1)
        earlier = jnp.where(first < second, 1.0, 0.0).astype(BF16)
        ranks = dot(jnp.where(mask, 1.0, 0.0).astype(BF16), earlier)
        rank = jnp.sum(jnp.where(mask, ranks, 0.0), axis=0, keepdims=True)
        return route.astype(F32) * float(cap) + rank

    def choose(r, k, target):
        slots = lax.broadcasted_iota(jnp.int32, (cap, rows), 0) + mates[k] * cap
        picks = jnp.where(slots.astype(F32) == target, 1.0, 0.0).astype(BF16)
        table[r, fixed(k), :] = picks
        held = sent if k else got
        held[r, fixed(k), :width] = dot(picks, tok[r]).astype(BF16)
        held[r, fixed(k), width:] = dot(picks, og[r]).astype(BF16)

    def dispatch_copy(r, k):
        return pltpu.make_async_remote_copy(
            src_ref=sent.at[r, fixed(k)],
            dst_ref=got.at[r, fixed(k)],
            send_sem=d_send.at[r, k],
            recv_sem=d_recv.at[r, k],
            device_id=(mates[k], node),
            device_id_type=MESH,
        )

    def return_copy(r, k):
        return pltpu.make_async_remote_copy(
            src_ref=back.at[r, fixed(k)],
            dst_ref=ret.at[r, fixed(k)],
            send_sem=r_send.at[r, k],
            recv_sem=r_recv.at[r, k],
            device_id=(mates[k], node),
            device_id_type=MESH,
        )

    def z_copy(r, way, j):
        return pltpu.make_async_remote_copy(
            src_ref=shared.at[r, bit(j)],
            dst_ref=beside.at[r, way, bit(j)],
            send_sem=z_send.at[r, way, j],
            recv_sem=z_recv.at[r, way, j],
            device_id=(expert, way * down + (1 - way) * up),
            device_id_type=MESH,
        )

    def x_copy(r, j):
        return pltpu.make_async_remote_copy(
            src_ref=pair.at[r, bit(j)],
            dst_ref=across.at[r, bit(j)],
            send_sem=x_send.at[r, j],
            recv_sem=x_recv.at[r, j],
            device_id=(expert, facing),
            device_id_type=MESH,
        )

    def start_return(r):
        for k in (2, 3, 1):
            return_copy(r, k).start()

    def slopes(r, half):
        part = pl.ds(half * rows, rows)
        pre = dot(got[r, part, :width], wide[...]) * factor
        grads = got[r, part, width:].astype(F32)
        slope[part, :] = (grads * 2.0 * jnp.maximum(pre, 0.0)).astype(BF16)

    def update_moment(r):
        def body(j, total):
            columns = pl.ds(pl.multiple_of(j * tile, tile), tile)
            grad = dot(got[r, :, columns], slope[...], 0, 0) * factor
            new = 0.9 * moment[strip(j), :] + grad
            moment[strip(j), :] = new
            return total + jnp.sum(new * new, axis=0, keepdims=True)

        total = lax.fori_loop(0, CHUNKS, body, jnp.zeros((1, hidden), F32))
        norm = jnp.sqrt(jnp.sum(total, axis=1, keepdims=True))
        scale = 1.0 / (norm + 1e-07)

        def scaled(j, carry):
            orthog[strip(j), :] = (moment[strip(j), :] * scale).astype(BF16)
            return carry

        lax.fori_loop(0, CHUNKS, scaled, 0)

    def polynomial():
        part = hidden // 2
        for i in range(2):
            columns = pl.ds(i * part, part)
            gram[columns, :] = dot(orthog[:, columns], orthog[...], 0, 0).astype(BF16)
        for i in range(2):
            columns = pl.ds(i * part, part)
            own = gram[columns, :]
            square = dot(own, gram[...])
            poly[columns, :] = (-4.775 * own.astype(F32) + 2.0315 * square).astype(BF16)

    def applied(j):
        own = orthog[strip(j), :]
        return (3.4445 * own.astype(F32) + dot(own, poly[...])).astype(BF16)

    def orthogonalize_and_share(r):
        def sweep(i, carry):
            polynomial()

            def body(j, inner):
                orthog[strip(j), :] = applied(j)
                return inner

            return lax.fori_loop(0, CHUNKS, body, carry)

        lax.fori_loop(0, NS_STEPS - 1, sweep, 0)
        polynomial()

        def last(j, carry):
            stepped = weight[strip(j), :] - step_size * applied(j).astype(F32)
            weight[strip(j), :] = stepped
            shared[r, strip(j), :] = stepped.astype(BF16)
            for i in range(PIECES // CHUNKS):
                z_copy(r, 0, j * (PIECES // CHUNKS) + i).start()
                z_copy(r, 1, j * (PIECES // CHUNKS) + i).start()
            return carry

        lax.fori_loop(0, CHUNKS, last, 0)

    def backward(r):
        for half in (1, 0):
            part = pl.ds(half * rows, rows)

            def body(j, carry, part=part):
                columns = pl.ds(pl.multiple_of(j * tile, tile), tile)
                grad = dot(slope[part, :], wide[strip(j), :], 1, 1) * factor
                back[r, part, columns] = grad.astype(BF16)
                return carry

            lax.fori_loop(0, CHUNKS, body, 0)
        ret[r, fixed(0), :] = back[r, fixed(0), :]

    def unsort(r):
        for k in (1, 2, 3):
            return_copy(r, k).wait_recv()

        def body(j, carry):
            columns = pl.ds(pl.multiple_of(j * tile, tile), tile)
            ig[r, :, columns] = dot(table[r], ret[r, :, columns], 0, 0).astype(BF16)
            return carry

        lax.fori_loop(0, CHUNKS, body, 0)

    def pass_across(r):
        def body(j, carry):
            z_copy(r, 1 - odd, j).wait_recv()
            own = shared[r, bit(j), :].astype(F32)
            pair[r, bit(j), :] = (own + beside[r, 1 - odd, bit(j), :].astype(F32)).astype(BF16)
            x_copy(r, j).start()
            return carry

        lax.fori_loop(0, PIECES, body, 0)

    def averaged(r, j):
        z_copy(r, odd, j).wait_recv()
        x_copy(r, j).wait_recv()
        neighbours = beside[r, 0, bit(j), :].astype(F32) + beside[r, 1, bit(j), :].astype(F32)
        neighbours = neighbours + across[r, bit(j), :].astype(F32)
        new = 0.4 * weight[bit(j), :] + 0.15 * neighbours
        weight[bit(j), :] = new
        return new

    load_route.wait()
    target = targets(0)
    loads[0].wait()
    loads[1].wait()
    for copy in (loads[2], loads[3], load_w, load_m):
        copy.start()
    choose(0, 2, target)
    pl.semaphore_wait(barrier, 6)
    dispatch_copy(0, 2).start()
    for k in (3, 1):
        choose(0, k, target)
        dispatch_copy(0, k).start()
    choose(0, 0, target)
    target = targets(1)
    loads[2].wait()
    loads[3].wait()
    for k in (2, 3, 1):
        choose(1, k, target)
        dispatch_copy(1, k).start()
    choose(1, 0, target)
    load_w.wait()

    def narrow(j, carry):
        wide[strip(j), :] = weight[strip(j), :].astype(BF16)
        return carry

    lax.fori_loop(0, CHUNKS, narrow, 0)
    load_m.wait()
    dispatch_copy(0, 1).wait_recv()
    slopes(0, 0)
    dispatch_copy(0, 2).wait_recv()
    dispatch_copy(0, 3).wait_recv()
    slopes(0, 1)
    update_moment(0)
    orthogonalize_and_share(0)
    backward(0)
    pass_across(0)
    start_return(0)

    def mixed(j, carry):
        wide[bit(j), :] = averaged(0, j).astype(BF16)
        return carry

    lax.fori_loop(0, PIECES, mixed, 0)

    for k in (1, 2, 3):
        dispatch_copy(1, k).wait_recv()
    slopes(1, 0)
    slopes(1, 1)
    backward(1)
    start_return(1)
    update_moment(1)
    orthogonalize_and_share(1)
    unsort(0)
    pass_across(1)
    unsort(1)

    def finished(j, carry):
        averaged(1, j)
        return carry

    lax.fori_loop(0, PIECES, finished, 0)

    for r in range(ROUNDS):
        for k in (1, 2, 3):
            dispatch_copy(r, k).wait_send()
            return_copy(r, k).wait_send()

        def sent_all(j, carry, r=r):
            z_copy(r, 0, j).wait_send()
            z_copy(r, 1, j).wait_send()
            x_copy(r, j).wait_send()
            return carry

        lax.fori_loop(0, PIECES, sent_all, 0)


def store(weight, moment, ig, w_out, m_out, ig_out, sems):
    copies = (
        pltpu.make_async_copy(weight, w_out.at[0, 0], sems.at[0]),
        pltpu.make_async_copy(moment, m_out.at[0, 0], sems.at[1]),
        pltpu.make_async_copy(ig, ig_out, sems.at[2]),
    )
    for copy in copies:
        copy.start()
    for copy in copies:
        copy.wait()


def on_device(tokens, routing, out_grad, weights, momentum):
    rounds, rows, width = tokens.shape
    hidden = out_grad.shape[2]
    experts = weights.shape[1] * lax.axis_size("expert")
    nodes = lax.axis_size("node")
    slots = experts * (rows // 2)
    anywhere = pl.BlockSpec(memory_space=pl.ANY)
    in_hbm = pl.BlockSpec(memory_space=pltpu.HBM)
    on_chip = pl.BlockSpec(memory_space=pltpu.VMEM)
    dma = pltpu.SemaphoreType.DMA
    operands = (
        pltpu.with_memory_space_constraint(x, pltpu.HBM)
        for x in (tokens, routing, out_grad, weights, momentum)
    )
    weight, moment, in_grad = pl.pallas_call(
        functools.partial(kernel, nodes),
        name="muon_rounds",
        out_shape=(
            pltpu.VMEM((width, hidden), F32),
            pltpu.VMEM((width, hidden), F32),
            pltpu.VMEM((rounds, rows, width), BF16),
        ),
        in_specs=[in_hbm] * 5,
        out_specs=(on_chip, on_chip, on_chip),
        scratch_shapes=[
            pltpu.VMEM((rounds, rows), jnp.int32),
            pltpu.VMEM((rounds, rows, width), BF16),
            pltpu.VMEM((rounds, rows, hidden), BF16),
            pltpu.VMEM((width, hidden), BF16),
            pltpu.VMEM((rounds, slots, rows), BF16),
            pltpu.VMEM((rounds, slots, width + hidden), BF16),
            pltpu.VMEM((rounds, slots, width + hidden), BF16),
            pltpu.VMEM((slots, hidden), BF16),
            pltpu.VMEM((width, hidden), BF16),
            pltpu.VMEM((hidden, hidden), BF16),
            pltpu.VMEM((hidden, hidden), BF16),
            pltpu.VMEM((rounds, slots, width), BF16),
            pltpu.VMEM((rounds, slots, width), BF16),
            pltpu.VMEM((rounds, width, hidden), BF16),
            pltpu.VMEM((rounds, 2, width, hidden), BF16),
            pltpu.VMEM((rounds, width, hidden), BF16),
            pltpu.VMEM((rounds, width, hidden), BF16),
            dma((7,)),
            dma((rounds, 4)),
            dma((rounds, 4)),
            dma((rounds, 4)),
            dma((rounds, 4)),
            dma((rounds, 2, PIECES)),
            dma((rounds, 2, PIECES)),
            dma((rounds, PIECES)),
            dma((rounds, PIECES)),
        ],
        compiler_params=pltpu.CompilerParams(
            collective_id=0, has_side_effects=True, vmem_limit_bytes=40 << 20
        ),
    )(*operands)
    return pl.pallas_call(
        store,
        name="store_results",
        out_shape=(
            jax.ShapeDtypeStruct(weights.shape, F32),
            jax.ShapeDtypeStruct(momentum.shape, F32),
            jax.ShapeDtypeStruct(tokens.shape, BF16),
        ),
        in_specs=[anywhere, anywhere, anywhere],
        out_specs=(anywhere, anywhere, anywhere),
        scratch_shapes=[dma((3,))],
        compiler_params=pltpu.CompilerParams(vmem_limit_bytes=1 << 20),
    )(weight, moment, in_grad)


def solution(mesh):
    return jax.shard_map(
        on_device,
        mesh=mesh,
        in_specs=(
            P(None, ("expert", "node"), None),
            P(None, ("expert", "node")),
            P(None, ("expert", "node"), None),
            P("node", "expert", None, None),
            P("node", "expert", None, None),
        ),
        out_specs=(
            P("node", "expert", None, None),
            P("node", "expert", None, None),
            P(None, ("expert", "node"), None),
        ),
        check_vma=False,
    )
```

```python
import functools
import math

import jax
import jax.numpy as jnp
from jax import lax
from jax.experimental import pallas as pl
from jax.experimental.pallas import tpu as pltpu
from jax.sharding import PartitionSpec as P

ROUNDS = 2
NS_STEPS = 3
CHUNKS = 4
PIECES = 8
MESH = pl.DeviceIdType.MESH
F32 = jnp.float32
BF16 = jnp.bfloat16


def dot(a, b, ca=1, cb=0):
    return lax.dot_general(a, b, (((ca,), (cb,)), ((), ())), preferred_element_type=F32)


def kernel(
    nodes,
    tok_hbm, route_hbm, og_hbm, w_hbm, m_hbm,
    weight, moment, ig,
    route_ref, tok, og, wide, table, sent, got, slope, orthog, gram, poly,
    back, ret, shared, beside, pair, across,
    in_sem, d_send, d_recv, r_send, r_recv, z_send, z_recv, x_send, x_recv, ready,
):
    expert = lax.axis_index("expert")
    node = lax.axis_index("node")
    rows, width = tok.shape[1], tok.shape[2]
    hidden = og.shape[2]
    cap = rows // 2
    tile = width // CHUNKS
    piece = width // PIECES
    factor = 1.0 / math.sqrt(width)
    step_size = 0.1 * math.sqrt(width)

    chip, core = expert // 2, expert % 2
    mates = (
        expert,
        2 * chip + (1 - core),
        2 * (1 - chip) + core,
        2 * (1 - chip) + (1 - core),
    )
    odd = node % 2
    up = (node + 2) % nodes
    down = (node + nodes - 2) % nodes
    facing = node + 1 - 2 * odd

    loads = []
    for r in range(ROUNDS):
        loads.append(pltpu.make_async_copy(tok_hbm.at[r], tok.at[r], in_sem.at[2 * r]))
        loads.append(pltpu.make_async_copy(og_hbm.at[r], og.at[r], in_sem.at[2 * r + 1]))
    load_w = pltpu.make_async_copy(w_hbm.at[0, 0], weight, in_sem.at[4])
    load_route = pltpu.make_async_copy(route_hbm, route_ref, in_sem.at[6])
    load_m = pltpu.make_async_copy(m_hbm.at[0, 0], moment, in_sem.at[5])
    for copy in (load_route, *loads[:2]):
        copy.start()

    barrier = pltpu.get_barrier_semaphore()
    for mate in mates[1:]:
        pl.semaphore_signal(barrier, inc=1, device_id=(mate, node), device_id_type=MESH)

    odd_z = (node // 2) % 2

    @pl.when(odd == 0)
    def _():
        pl.semaphore_signal(barrier, inc=1, device_id=(expert, facing), device_id_type=MESH)

    @pl.when(odd_z == 0)
    def _():
        for other in (up, down):
            pl.semaphore_signal(barrier, inc=1, device_id=(expert, other), device_id_type=MESH)

    def fixed(index):
        return pl.ds(index * cap, cap)

    def strip(index):
        return pl.ds(pl.multiple_of(index * tile, tile), tile)

    def bit(index):
        return pl.ds(pl.multiple_of(index * piece, piece), piece)

    def targets(r):
        route = route_ref[r : r + 1, :]
        mask = lax.broadcasted_iota(jnp.int32, (16, rows), 0) == route
        first = lax.broadcasted_iota(jnp.int32, (rows, rows), 0)
        second = lax.broadcasted_iota(jnp.int32, (rows, rows), 1)
        earlier = jnp.where(first < second, 1.0, 0.0).astype(BF16)
        ranks = dot(jnp.where(mask, 1.0, 0.0).astype(BF16), earlier)
        rank = jnp.sum(jnp.where(mask, ranks, 0.0), axis=0, keepdims=True)
        return route.astype(F32) * float(cap) + rank

    def choose(r, k, target):
        slots = lax.broadcasted_iota(jnp.int32, (cap, rows), 0) + mates[k] * cap
        picks = jnp.where(slots.astype(F32) == target, 1.0, 0.0).astype(BF16)
        table[r, fixed(k), :] = picks
        held = sent if k else got
        held[r, fixed(k), :width] = dot(picks, tok[r]).astype(BF16)
        held[r, fixed(k), width:] = dot(picks, og[r]).astype(BF16)

    def dispatch_copy(r, k):
        return pltpu.make_async_remote_copy(
            src_ref=sent.at[r, fixed(k)],
            dst_ref=got.at[r, fixed(k)],
            send_sem=d_send.at[r, k],
            recv_sem=d_recv.at[r, k],
            device_id=(mates[k], node),
            device_id_type=MESH,
        )

    def return_copy(r, k):
        return pltpu.make_async_remote_copy(
            src_ref=back.at[r, fixed(k)],
            dst_ref=ret.at[r, fixed(k)],
            send_sem=r_send.at[r, k],
            recv_sem=r_recv.at[r, k],
            device_id=(mates[k], node),
            device_id_type=MESH,
        )

    def z_copy(r, way, j):
        return pltpu.make_async_remote_copy(
            src_ref=shared.at[r, bit(j)],
            dst_ref=beside.at[r, way, bit(j)],
            send_sem=z_send.at[r, way, j],
            recv_sem=z_recv.at[r, way, j],
            device_id=(expert, way * down + (1 - way) * up),
            device_id_type=MESH,
        )

    def x_copy(r, j):
        return pltpu.make_async_remote_copy(
            src_ref=pair.at[r, bit(j)],
            dst_ref=across.at[r, bit(j)],
            send_sem=x_send.at[r, j],
            recv_sem=x_recv.at[r, j],
            device_id=(expert, facing),
            device_id_type=MESH,
        )

    def start_return(r):
        for k in (2, 3, 1):
            return_copy(r, k).start()

    def slopes(r, half):
        part = pl.ds(half * rows, rows)
        pre = dot(got[r, part, :width], wide[...]) * factor
        grads = got[r, part, width:].astype(F32)
        slope[part, :] = (grads * 2.0 * jnp.maximum(pre, 0.0)).astype(BF16)

    def update_moment(r):
        def body(j, total):
            columns = pl.ds(pl.multiple_of(j * tile, tile), tile)
            grad = dot(got[r, :, columns], slope[...], 0, 0) * factor
            new = 0.9 * moment[strip(j), :] + grad
            moment[strip(j), :] = new
            return total + jnp.sum(new * new, axis=0, keepdims=True)

        total = lax.fori_loop(0, CHUNKS, body, jnp.zeros((1, hidden), F32))
        norm = jnp.sqrt(jnp.sum(total, axis=1, keepdims=True))
        scale = 1.0 / (norm + 1e-07)

        def scaled(j, carry):
            orthog[strip(j), :] = (moment[strip(j), :] * scale).astype(BF16)
            return carry

        lax.fori_loop(0, CHUNKS, scaled, 0)

    def polynomial():
        part = hidden // 2
        for i in range(2):
            columns = pl.ds(i * part, part)
            gram[columns, :] = dot(orthog[:, columns], orthog[...], 0, 0).astype(BF16)
        for i in range(2):
            columns = pl.ds(i * part, part)
            own = gram[columns, :]
            square = dot(own, gram[...])
            poly[columns, :] = (-4.775 * own.astype(F32) + 2.0315 * square).astype(BF16)

    def applied(j):
        own = orthog[strip(j), :]
        return (3.4445 * own.astype(F32) + dot(own, poly[...])).astype(BF16)

    def orthogonalize_and_share(r):
        def sweep(i, carry):
            polynomial()

            def body(j, inner):
                orthog[strip(j), :] = applied(j)
                return inner

            return lax.fori_loop(0, CHUNKS, body, carry)

        lax.fori_loop(0, NS_STEPS - 1, sweep, 0)
        polynomial()

        def last(j, carry):
            stepped = weight[strip(j), :] - step_size * applied(j).astype(F32)
            weight[strip(j), :] = stepped
            shared[r, strip(j), :] = stepped.astype(BF16)
            for i in range(PIECES // CHUNKS):
                z_copy(r, 0, j * (PIECES // CHUNKS) + i).start()
                z_copy(r, 1, j * (PIECES // CHUNKS) + i).start()
            return carry

        lax.fori_loop(0, CHUNKS, last, 0)

    def backward(r):
        for half in (1, 0):
            part = pl.ds(half * rows, rows)

            def body(j, carry, part=part):
                columns = pl.ds(pl.multiple_of(j * tile, tile), tile)
                grad = dot(slope[part, :], wide[strip(j), :], 1, 1) * factor
                back[r, part, columns] = grad.astype(BF16)
                return carry

            lax.fori_loop(0, CHUNKS, body, 0)
        ret[r, fixed(0), :] = back[r, fixed(0), :]

    def unsort(r):
        for k in (1, 2, 3):
            return_copy(r, k).wait_recv()

        def body(j, carry):
            columns = pl.ds(pl.multiple_of(j * tile, tile), tile)
            ig[r, :, columns] = dot(table[r], ret[r, :, columns], 0, 0).astype(BF16)
            return carry

        lax.fori_loop(0, CHUNKS, body, 0)

    def pass_across(r):
        def body(j, carry):
            z_copy(r, 1 - odd, j).wait_recv()
            own = shared[r, bit(j), :].astype(F32)
            pair[r, bit(j), :] = (own + beside[r, 1 - odd, bit(j), :].astype(F32)).astype(BF16)
            x_copy(r, j).start()
            return carry

        lax.fori_loop(0, PIECES, body, 0)

    def averaged(r, j):
        z_copy(r, odd, j).wait_recv()
        x_copy(r, j).wait_recv()
        neighbours = beside[r, 0, bit(j), :].astype(F32) + beside[r, 1, bit(j), :].astype(F32)
        neighbours = neighbours + across[r, bit(j), :].astype(F32)
        new = 0.4 * weight[bit(j), :] + 0.15 * neighbours
        weight[bit(j), :] = new
        return new

    load_route.wait()
    target = targets(0)
    loads[0].wait()
    loads[1].wait()
    for copy in (loads[2], loads[3], load_w, load_m):
        copy.start()
    choose(0, 2, target)
    pl.semaphore_wait(barrier, 3 + odd + 2 * odd_z)

    @pl.when(odd_z == 1)
    def _():
        for other in (up, down):
            pl.semaphore_signal(ready.at[0], inc=1, device_id=(expert, other), device_id_type=MESH)

    @pl.when(odd == 1)
    def _():
        pl.semaphore_signal(ready.at[1], inc=1, device_id=(expert, facing), device_id_type=MESH)

    dispatch_copy(0, 2).start()
    for k in (3, 1):
        choose(0, k, target)
        dispatch_copy(0, k).start()
    choose(0, 0, target)
    target = targets(1)
    loads[2].wait()
    loads[3].wait()
    for k in (2, 3, 1):
        choose(1, k, target)
        dispatch_copy(1, k).start()
    choose(1, 0, target)
    load_w.wait()

    def narrow(j, carry):
        wide[strip(j), :] = weight[strip(j), :].astype(BF16)
        return carry

    lax.fori_loop(0, CHUNKS, narrow, 0)
    load_m.wait()
    dispatch_copy(0, 1).wait_recv()
    slopes(0, 0)
    dispatch_copy(0, 2).wait_recv()
    dispatch_copy(0, 3).wait_recv()
    slopes(0, 1)
    update_moment(0)

    @pl.when(odd_z == 0)
    def _():
        pl.semaphore_wait(ready.at[0], 2)

    orthogonalize_and_share(0)
    backward(0)

    @pl.when(odd == 0)
    def _():
        pl.semaphore_wait(ready.at[1], 1)

    pass_across(0)
    start_return(0)

    def mixed(j, carry):
        wide[bit(j), :] = averaged(0, j).astype(BF16)
        return carry

    lax.fori_loop(0, PIECES, mixed, 0)

    for k in (1, 2, 3):
        dispatch_copy(1, k).wait_recv()
    slopes(1, 0)
    slopes(1, 1)
    backward(1)
    start_return(1)
    update_moment(1)
    orthogonalize_and_share(1)
    unsort(0)
    pass_across(1)
    unsort(1)

    def finished(j, carry):
        averaged(1, j)
        return carry

    lax.fori_loop(0, PIECES, finished, 0)

    for r in range(ROUNDS):
        for k in (1, 2, 3):
            dispatch_copy(r, k).wait_send()
            return_copy(r, k).wait_send()

        def sent_all(j, carry, r=r):
            z_copy(r, 0, j).wait_send()
            z_copy(r, 1, j).wait_send()
            x_copy(r, j).wait_send()
            return carry

        lax.fori_loop(0, PIECES, sent_all, 0)


def store(weight, moment, ig, w_out, m_out, ig_out, sems):
    copies = (
        pltpu.make_async_copy(weight, w_out.at[0, 0], sems.at[0]),
        pltpu.make_async_copy(moment, m_out.at[0, 0], sems.at[1]),
        pltpu.make_async_copy(ig, ig_out, sems.at[2]),
    )
    for copy in copies:
        copy.start()
    for copy in copies:
        copy.wait()


def on_device(tokens, routing, out_grad, weights, momentum):
    rounds, rows, width = tokens.shape
    hidden = out_grad.shape[2]
    experts = weights.shape[1] * lax.axis_size("expert")
    nodes = lax.axis_size("node")
    slots = experts * (rows // 2)
    anywhere = pl.BlockSpec(memory_space=pl.ANY)
    in_hbm = pl.BlockSpec(memory_space=pltpu.HBM)
    on_chip = pl.BlockSpec(memory_space=pltpu.VMEM)
    dma = pltpu.SemaphoreType.DMA
    operands = (
        pltpu.with_memory_space_constraint(x, pltpu.HBM)
        for x in (tokens, routing, out_grad, weights, momentum)
    )
    weight, moment, in_grad = pl.pallas_call(
        functools.partial(kernel, nodes),
        name="muon_rounds",
        out_shape=(
            pltpu.VMEM((width, hidden), F32),
            pltpu.VMEM((width, hidden), F32),
            pltpu.VMEM((rounds, rows, width), BF16),
        ),
        in_specs=[in_hbm] * 5,
        out_specs=(on_chip, on_chip, on_chip),
        scratch_shapes=[
            pltpu.VMEM((rounds, rows), jnp.int32),
            pltpu.VMEM((rounds, rows, width), BF16),
            pltpu.VMEM((rounds, rows, hidden), BF16),
            pltpu.VMEM((width, hidden), BF16),
            pltpu.VMEM((rounds, slots, rows), BF16),
            pltpu.VMEM((rounds, slots, width + hidden), BF16),
            pltpu.VMEM((rounds, slots, width + hidden), BF16),
            pltpu.VMEM((slots, hidden), BF16),
            pltpu.VMEM((width, hidden), BF16),
            pltpu.VMEM((hidden, hidden), BF16),
            pltpu.VMEM((hidden, hidden), BF16),
            pltpu.VMEM((rounds, slots, width), BF16),
            pltpu.VMEM((rounds, slots, width), BF16),
            pltpu.VMEM((rounds, width, hidden), BF16),
            pltpu.VMEM((rounds, 2, width, hidden), BF16),
            pltpu.VMEM((rounds, width, hidden), BF16),
            pltpu.VMEM((rounds, width, hidden), BF16),
            dma((7,)),
            dma((rounds, 4)),
            dma((rounds, 4)),
            dma((rounds, 4)),
            dma((rounds, 4)),
            dma((rounds, 2, PIECES)),
            dma((rounds, 2, PIECES)),
            dma((rounds, PIECES)),
            dma((rounds, PIECES)),
            pltpu.SemaphoreType.REGULAR((2,)),
        ],
        compiler_params=pltpu.CompilerParams(
            collective_id=0, has_side_effects=True, vmem_limit_bytes=40 << 20
        ),
    )(*operands)
    return pl.pallas_call(
        store,
        name="store_results",
        out_shape=(
            jax.ShapeDtypeStruct(weights.shape, F32),
            jax.ShapeDtypeStruct(momentum.shape, F32),
            jax.ShapeDtypeStruct(tokens.shape, BF16),
        ),
        in_specs=[anywhere, anywhere, anywhere],
        out_specs=(anywhere, anywhere, anywhere),
        scratch_shapes=[dma((3,))],
        compiler_params=pltpu.CompilerParams(vmem_limit_bytes=1 << 20),
    )(weight, moment, in_grad)


def solution(mesh):
    return jax.shard_map(
        on_device,
        mesh=mesh,
        in_specs=(
            P(None, ("expert", "node"), None),
            P(None, ("expert", "node")),
            P(None, ("expert", "node"), None),
            P("node", "expert", None, None),
            P("node", "expert", None, None),
        ),
        out_specs=(
            P("node", "expert", None, None),
            P("node", "expert", None, None),
            P(None, ("expert", "node"), None),
        ),
        check_vma=False,
    )
```

```python
import functools
import math

import jax
import jax.numpy as jnp
from jax import lax
from jax.experimental import pallas as pl
from jax.experimental.pallas import tpu as pltpu
from jax.sharding import PartitionSpec as P

ROUNDS = 2
NS_STEPS = 3
CHUNKS = 4
PIECES = 8
MESH = pl.DeviceIdType.MESH
F32 = jnp.float32
BF16 = jnp.bfloat16


def dot(a, b, ca=1, cb=0):
    return lax.dot_general(a, b, (((ca,), (cb,)), ((), ())), preferred_element_type=F32)


def kernel(
    nodes,
    tok_hbm, route_hbm, og_hbm, w_hbm, m_hbm,
    weight, moment, ig,
    route_ref, tok, og, wide, table, sent, got, slope, orthog, gram, poly,
    back, ret, shared, beside, pair, across,
    in_sem, d_send, d_recv, r_send, r_recv, z_send, z_recv, x_send, x_recv, ready,
):
    expert = lax.axis_index("expert")
    node = lax.axis_index("node")
    rows, width = tok.shape[1], tok.shape[2]
    hidden = og.shape[2]
    cap = rows // 2
    tile = width // CHUNKS
    piece = width // PIECES
    factor = 1.0 / math.sqrt(width)
    step_size = 0.1 * math.sqrt(width)

    chip, core = expert // 2, expert % 2
    mates = (
        expert,
        2 * chip + (1 - core),
        2 * (1 - chip) + core,
        2 * (1 - chip) + (1 - core),
    )
    odd = node % 2
    up = (node + 2) % nodes
    down = (node + nodes - 2) % nodes
    facing = node + 1 - 2 * odd

    loads = []
    for r in range(ROUNDS):
        loads.append(pltpu.make_async_copy(tok_hbm.at[r], tok.at[r], in_sem.at[2 * r]))
        loads.append(pltpu.make_async_copy(og_hbm.at[r], og.at[r], in_sem.at[2 * r + 1]))
    load_w = pltpu.make_async_copy(w_hbm.at[0, 0], weight, in_sem.at[4])
    load_route = pltpu.make_async_copy(route_hbm, route_ref, in_sem.at[6])
    load_m = pltpu.make_async_copy(m_hbm.at[0, 0], moment, in_sem.at[5])
    for copy in (load_route, *loads[:2]):
        copy.start()

    barrier = pltpu.get_barrier_semaphore()
    for mate in mates[1:]:
        pl.semaphore_signal(barrier, inc=1, device_id=(mate, node), device_id_type=MESH)

    odd_z = (node // 2) % 2

    @pl.when(odd == 0)
    def _():
        pl.semaphore_signal(barrier, inc=1, device_id=(expert, facing), device_id_type=MESH)

    @pl.when(odd_z == 0)
    def _():
        for other in (up, down):
            pl.semaphore_signal(barrier, inc=1, device_id=(expert, other), device_id_type=MESH)

    def fixed(index):
        return pl.ds(index * cap, cap)

    def strip(index):
        return pl.ds(pl.multiple_of(index * tile, tile), tile)

    def bit(index):
        return pl.ds(pl.multiple_of(index * piece, piece), piece)

    def targets(r):
        route = route_ref[r : r + 1, :]
        mask = lax.broadcasted_iota(jnp.int32, (16, rows), 0) == route
        first = lax.broadcasted_iota(jnp.int32, (rows, rows), 0)
        second = lax.broadcasted_iota(jnp.int32, (rows, rows), 1)
        earlier = jnp.where(first < second, 1.0, 0.0).astype(BF16)
        ranks = dot(jnp.where(mask, 1.0, 0.0).astype(BF16), earlier)
        rank = jnp.sum(jnp.where(mask, ranks, 0.0), axis=0, keepdims=True)
        return route.astype(F32) * float(cap) + rank

    def choose(r, k, target):
        slots = lax.broadcasted_iota(jnp.int32, (cap, rows), 0) + mates[k] * cap
        picks = jnp.where(slots.astype(F32) == target, 1.0, 0.0).astype(BF16)
        table[r, fixed(k), :] = picks
        held = sent if k else got
        held[r, fixed(k), :width] = dot(picks, tok[r]).astype(BF16)
        held[r, fixed(k), width:] = dot(picks, og[r]).astype(BF16)

    def dispatch_copy(r, k):
        return pltpu.make_async_remote_copy(
            src_ref=sent.at[r, fixed(k)],
            dst_ref=got.at[r, fixed(k)],
            send_sem=d_send.at[r, k],
            recv_sem=d_recv.at[r, k],
            device_id=(mates[k], node),
            device_id_type=MESH,
        )

    def return_copy(r, k, part):
        some = pl.ds(k * cap + part * (cap // 2), cap // 2)
        return pltpu.make_async_remote_copy(
            src_ref=back.at[r, some],
            dst_ref=ret.at[r, some],
            send_sem=r_send.at[r, k, part],
            recv_sem=r_recv.at[r, k, part],
            device_id=(mates[k], node),
            device_id_type=MESH,
        )

    def z_copy(r, way, j):
        return pltpu.make_async_remote_copy(
            src_ref=shared.at[r, bit(j)],
            dst_ref=beside.at[r, way, bit(j)],
            send_sem=z_send.at[r, way, j],
            recv_sem=z_recv.at[r, way, j],
            device_id=(expert, way * down + (1 - way) * up),
            device_id_type=MESH,
        )

    def x_copy(r, j):
        return pltpu.make_async_remote_copy(
            src_ref=pair.at[r, bit(j)],
            dst_ref=across.at[r, bit(j)],
            send_sem=x_send.at[r, j],
            recv_sem=x_recv.at[r, j],
            device_id=(expert, facing),
            device_id_type=MESH,
        )

    def start_return(r, k):
        for part in range(2):
            return_copy(r, k, part).start()

    def slopes(r, half):
        part = pl.ds(half * rows, rows)
        pre = dot(got[r, part, :width], wide[...]) * factor
        grads = got[r, part, width:].astype(F32)
        slope[part, :] = (grads * 2.0 * jnp.maximum(pre, 0.0)).astype(BF16)

    def update_moment(r):
        def body(j, total):
            columns = pl.ds(pl.multiple_of(j * tile, tile), tile)
            grad = dot(got[r, :, columns], slope[...], 0, 0) * factor
            new = 0.9 * moment[strip(j), :] + grad
            moment[strip(j), :] = new
            return total + jnp.sum(new * new, axis=0, keepdims=True)

        total = lax.fori_loop(0, CHUNKS, body, jnp.zeros((1, hidden), F32))
        norm = jnp.sqrt(jnp.sum(total, axis=1, keepdims=True))
        scale = 1.0 / (norm + 1e-07)

        def scaled(j, carry):
            orthog[strip(j), :] = (moment[strip(j), :] * scale).astype(BF16)
            return carry

        lax.fori_loop(0, CHUNKS, scaled, 0)

    def polynomial():
        part = hidden // 2
        for i in range(2):
            columns = pl.ds(i * part, part)
            gram[columns, :] = dot(orthog[:, columns], orthog[...], 0, 0).astype(BF16)
        for i in range(2):
            columns = pl.ds(i * part, part)
            own = gram[columns, :]
            square = dot(own, gram[...])
            poly[columns, :] = (-4.775 * own.astype(F32) + 2.0315 * square).astype(BF16)

    def applied(j):
        own = orthog[strip(j), :]
        return (3.4445 * own.astype(F32) + dot(own, poly[...])).astype(BF16)

    def orthogonalize_and_share(r):
        def sweep(i, carry):
            polynomial()

            def body(j, inner):
                orthog[strip(j), :] = applied(j)
                return inner

            return lax.fori_loop(0, CHUNKS, body, carry)

        lax.fori_loop(0, NS_STEPS - 1, sweep, 0)
        polynomial()

        def last(j, carry):
            stepped = weight[strip(j), :] - step_size * applied(j).astype(F32)
            weight[strip(j), :] = stepped
            shared[r, strip(j), :] = stepped.astype(BF16)
            for i in range(PIECES // CHUNKS):
                z_copy(r, 0, j * (PIECES // CHUNKS) + i).start()
                z_copy(r, 1, j * (PIECES // CHUNKS) + i).start()
            return carry

        lax.fori_loop(0, CHUNKS, last, 0)

    def backward(r, k, blocks):
        part = pl.ds(k * cap, blocks * cap)

        def body(j, carry):
            columns = pl.ds(pl.multiple_of(j * tile, tile), tile)
            grad = dot(slope[part, :], wide[strip(j), :], 1, 1) * factor
            back[r, part, columns] = grad.astype(BF16)
            return carry

        lax.fori_loop(0, CHUNKS, body, 0)
        if k == 0:
            ret[r, fixed(0), :] = back[r, fixed(0), :]

    def unsort(r, k, blocks):
        for i in range(max(k, 1), k + blocks):
            return_copy(r, i, 0).wait_recv()
            return_copy(r, i, 1).wait_recv()
        part = pl.ds(k * cap, blocks * cap)

        def body(j, carry):
            columns = pl.ds(pl.multiple_of(j * tile, tile), tile)
            placed = dot(table[r, part, :], ret[r, part, columns], 0, 0)
            if k:
                placed = placed + ig[r, :, columns].astype(F32)
            ig[r, :, columns] = placed.astype(BF16)
            return carry

        lax.fori_loop(0, CHUNKS, body, 0)

    def pass_across(r, first, last):
        def body(j, carry):
            z_copy(r, 1 - odd, j).wait_recv()
            own = shared[r, bit(j), :].astype(F32)
            pair[r, bit(j), :] = (own + beside[r, 1 - odd, bit(j), :].astype(F32)).astype(BF16)
            x_copy(r, j).start()
            return carry

        lax.fori_loop(first, last, body, 0)

    def averaged(r, j):
        z_copy(r, odd, j).wait_recv()
        x_copy(r, j).wait_recv()
        neighbours = beside[r, 0, bit(j), :].astype(F32) + beside[r, 1, bit(j), :].astype(F32)
        neighbours = neighbours + across[r, bit(j), :].astype(F32)
        new = 0.4 * weight[bit(j), :] + 0.15 * neighbours
        weight[bit(j), :] = new
        return new

    load_route.wait()
    target = targets(0)
    loads[0].wait()
    loads[1].wait()
    for copy in (loads[2], loads[3], load_w, load_m):
        copy.start()
    choose(0, 2, target)
    pl.semaphore_wait(barrier, 3 + odd + 2 * odd_z)

    @pl.when(odd_z == 1)
    def _():
        for other in (up, down):
            pl.semaphore_signal(ready.at[0], inc=1, device_id=(expert, other), device_id_type=MESH)

    @pl.when(odd == 1)
    def _():
        pl.semaphore_signal(ready.at[1], inc=1, device_id=(expert, facing), device_id_type=MESH)

    dispatch_copy(0, 2).start()
    for k in (3, 1):
        choose(0, k, target)
        dispatch_copy(0, k).start()
    choose(0, 0, target)
    target = targets(1)
    loads[2].wait()
    loads[3].wait()
    for k in (2, 3, 1):
        choose(1, k, target)
        dispatch_copy(1, k).start()
    choose(1, 0, target)
    load_w.wait()

    def narrow(j, carry):
        wide[strip(j), :] = weight[strip(j), :].astype(BF16)
        return carry

    lax.fori_loop(0, CHUNKS, narrow, 0)
    load_m.wait()
    dispatch_copy(0, 1).wait_recv()
    slopes(0, 0)
    dispatch_copy(0, 2).wait_recv()
    dispatch_copy(0, 3).wait_recv()
    slopes(0, 1)
    update_moment(0)

    @pl.when(odd_z == 0)
    def _():
        pl.semaphore_wait(ready.at[0], 2)

    orthogonalize_and_share(0)
    backward(0, 2, 2)
    backward(0, 0, 2)

    @pl.when(odd == 0)
    def _():
        pl.semaphore_wait(ready.at[1], 1)

    pass_across(0, 0, PIECES)
    for k in (2, 3, 1):
        start_return(0, k)

    def mixed(j, carry):
        wide[bit(j), :] = averaged(0, j).astype(BF16)
        return carry

    lax.fori_loop(0, PIECES, mixed, 0)

    for k in (1, 2, 3):
        dispatch_copy(1, k).wait_recv()
    slopes(1, 0)
    slopes(1, 1)
    backward(1, 2, 1)
    start_return(1, 2)
    update_moment(1)
    orthogonalize_and_share(1)
    backward(1, 3, 1)
    backward(1, 0, 2)
    start_return(1, 1)
    pass_across(1, 0, PIECES // 2)
    return_copy(1, 3, 0).start()
    unsort(0, 0, 4)
    pass_across(1, PIECES // 2, PIECES)
    return_copy(1, 3, 1).start()
    unsort(1, 0, 3)

    def finished(j, carry):
        averaged(1, j)
        return carry

    lax.fori_loop(0, PIECES, finished, 0)
    unsort(1, 3, 1)

    for r in range(ROUNDS):
        for k in (1, 2, 3):
            dispatch_copy(r, k).wait_send()
            return_copy(r, k, 0).wait_send()
            return_copy(r, k, 1).wait_send()

        def sent_all(j, carry, r=r):
            z_copy(r, 0, j).wait_send()
            z_copy(r, 1, j).wait_send()
            x_copy(r, j).wait_send()
            return carry

        lax.fori_loop(0, PIECES, sent_all, 0)


def store(weight, moment, ig, w_out, m_out, ig_out, sems):
    copies = (
        pltpu.make_async_copy(weight, w_out.at[0, 0], sems.at[0]),
        pltpu.make_async_copy(moment, m_out.at[0, 0], sems.at[1]),
        pltpu.make_async_copy(ig, ig_out, sems.at[2]),
    )
    for copy in copies:
        copy.start()
    for copy in copies:
        copy.wait()


def on_device(tokens, routing, out_grad, weights, momentum):
    rounds, rows, width = tokens.shape
    hidden = out_grad.shape[2]
    experts = weights.shape[1] * lax.axis_size("expert")
    nodes = lax.axis_size("node")
    slots = experts * (rows // 2)
    anywhere = pl.BlockSpec(memory_space=pl.ANY)
    in_hbm = pl.BlockSpec(memory_space=pltpu.HBM)
    on_chip = pl.BlockSpec(memory_space=pltpu.VMEM)
    dma = pltpu.SemaphoreType.DMA
    operands = (
        pltpu.with_memory_space_constraint(x, pltpu.HBM)
        for x in (tokens, routing, out_grad, weights, momentum)
    )
    weight, moment, in_grad = pl.pallas_call(
        functools.partial(kernel, nodes),
        name="muon_rounds",
        out_shape=(
            pltpu.VMEM((width, hidden), F32),
            pltpu.VMEM((width, hidden), F32),
            pltpu.VMEM((rounds, rows, width), BF16),
        ),
        in_specs=[in_hbm] * 5,
        out_specs=(on_chip, on_chip, on_chip),
        scratch_shapes=[
            pltpu.VMEM((rounds, rows), jnp.int32),
            pltpu.VMEM((rounds, rows, width), BF16),
            pltpu.VMEM((rounds, rows, hidden), BF16),
            pltpu.VMEM((width, hidden), BF16),
            pltpu.VMEM((rounds, slots, rows), BF16),
            pltpu.VMEM((rounds, slots, width + hidden), BF16),
            pltpu.VMEM((rounds, slots, width + hidden), BF16),
            pltpu.VMEM((slots, hidden), BF16),
            pltpu.VMEM((width, hidden), BF16),
            pltpu.VMEM((hidden, hidden), BF16),
            pltpu.VMEM((hidden, hidden), BF16),
            pltpu.VMEM((rounds, slots, width), BF16),
            pltpu.VMEM((rounds, slots, width), BF16),
            pltpu.VMEM((rounds, width, hidden), BF16),
            pltpu.VMEM((rounds, 2, width, hidden), BF16),
            pltpu.VMEM((rounds, width, hidden), BF16),
            pltpu.VMEM((rounds, width, hidden), BF16),
            dma((7,)),
            dma((rounds, 4)),
            dma((rounds, 4)),
            dma((rounds, 4, 2)),
            dma((rounds, 4, 2)),
            dma((rounds, 2, PIECES)),
            dma((rounds, 2, PIECES)),
            dma((rounds, PIECES)),
            dma((rounds, PIECES)),
            pltpu.SemaphoreType.REGULAR((2,)),
        ],
        compiler_params=pltpu.CompilerParams(
            collective_id=0, has_side_effects=True, vmem_limit_bytes=40 << 20
        ),
    )(*operands)
    return pl.pallas_call(
        store,
        name="store_results",
        out_shape=(
            jax.ShapeDtypeStruct(weights.shape, F32),
            jax.ShapeDtypeStruct(momentum.shape, F32),
            jax.ShapeDtypeStruct(tokens.shape, BF16),
        ),
        in_specs=[anywhere, anywhere, anywhere],
        out_specs=(anywhere, anywhere, anywhere),
        scratch_shapes=[dma((3,))],
        compiler_params=pltpu.CompilerParams(vmem_limit_bytes=1 << 20),
    )(weight, moment, in_grad)


def solution(mesh):
    return jax.shard_map(
        on_device,
        mesh=mesh,
        in_specs=(
            P(None, ("expert", "node"), None),
            P(None, ("expert", "node")),
            P(None, ("expert", "node"), None),
            P("node", "expert", None, None),
            P("node", "expert", None, None),
        ),
        out_specs=(
            P("node", "expert", None, None),
            P("node", "expert", None, None),
            P(None, ("expert", "node"), None),
        ),
        check_vma=False,
    )
```

```python
import functools
import math

import jax
import jax.numpy as jnp
from jax import lax
from jax.experimental import pallas as pl
from jax.experimental.pallas import tpu as pltpu
from jax.sharding import PartitionSpec as P

ROUNDS = 2
NS_STEPS = 3
CHUNKS = 4
PIECES = 8
MESH = pl.DeviceIdType.MESH
F32 = jnp.float32
BF16 = jnp.bfloat16


def dot(a, b, ca=1, cb=0):
    return lax.dot_general(a, b, (((ca,), (cb,)), ((), ())), preferred_element_type=F32)


def kernel(
    nodes,
    tok_hbm, route_hbm, og_hbm, w_hbm, m_hbm,
    weight, moment, ig,
    route_ref, tok, og, wide, table, sent, got, slope, orthog, gram, poly,
    back, ret, shared, beside, pair, across,
    in_sem, d_send, d_recv, r_send, r_recv, z_send, z_recv, x_send, x_recv, ready,
):
    expert = lax.axis_index("expert")
    node = lax.axis_index("node")
    rows, width = tok.shape[1], tok.shape[2]
    hidden = og.shape[2]
    cap = rows // 2
    tile = width // CHUNKS
    piece = width // PIECES
    factor = 1.0 / math.sqrt(width)
    step_size = 0.1 * math.sqrt(width)

    chip, core = expert // 2, expert % 2
    mates = (
        expert,
        2 * chip + (1 - core),
        2 * (1 - chip) + core,
        2 * (1 - chip) + (1 - core),
    )
    odd = node % 2
    up = (node + 2) % nodes
    down = (node + nodes - 2) % nodes
    facing = node + 1 - 2 * odd

    loads = []
    for r in range(ROUNDS):
        loads.append(pltpu.make_async_copy(tok_hbm.at[r], tok.at[r], in_sem.at[2 * r]))
        loads.append(pltpu.make_async_copy(og_hbm.at[r], og.at[r], in_sem.at[2 * r + 1]))
    load_w = pltpu.make_async_copy(w_hbm.at[0, 0], weight, in_sem.at[4])
    load_route = pltpu.make_async_copy(route_hbm, route_ref, in_sem.at[6])
    load_m = pltpu.make_async_copy(m_hbm.at[0, 0], moment, in_sem.at[5])
    for copy in (load_route, *loads[:2]):
        copy.start()

    barrier = pltpu.get_barrier_semaphore()
    for mate in mates[1:]:
        pl.semaphore_signal(barrier, inc=1, device_id=(mate, node), device_id_type=MESH)

    odd_z = (node // 2) % 2

    @pl.when(odd == 0)
    def _():
        pl.semaphore_signal(barrier, inc=1, device_id=(expert, facing), device_id_type=MESH)

    @pl.when(odd_z == 0)
    def _():
        for other in (up, down):
            pl.semaphore_signal(barrier, inc=1, device_id=(expert, other), device_id_type=MESH)

    def fixed(index):
        return pl.ds(index * cap, cap)

    def strip(index):
        return pl.ds(pl.multiple_of(index * tile, tile), tile)

    def bit(index):
        return pl.ds(pl.multiple_of(index * piece, piece), piece)

    def targets(r):
        route = route_ref[r : r + 1, :]
        mask = lax.broadcasted_iota(jnp.int32, (16, rows), 0) == route
        first = lax.broadcasted_iota(jnp.int32, (rows, rows), 0)
        second = lax.broadcasted_iota(jnp.int32, (rows, rows), 1)
        earlier = jnp.where(first < second, 1.0, 0.0).astype(BF16)
        ranks = dot(jnp.where(mask, 1.0, 0.0).astype(BF16), earlier)
        rank = jnp.sum(jnp.where(mask, ranks, 0.0), axis=0, keepdims=True)
        return route.astype(F32) * float(cap) + rank

    def choose(r, k, target):
        slots = lax.broadcasted_iota(jnp.int32, (cap, rows), 0) + mates[k] * cap
        picks = jnp.where(slots.astype(F32) == target, 1.0, 0.0).astype(BF16)
        table[r, fixed(k), :] = picks
        held = sent if k else got
        held[r, fixed(k), :width] = dot(picks, tok[r]).astype(BF16)
        held[r, fixed(k), width:] = dot(picks, og[r]).astype(BF16)

    def dispatch_copy(r, k):
        return pltpu.make_async_remote_copy(
            src_ref=sent.at[r, fixed(k)],
            dst_ref=got.at[r, fixed(k)],
            send_sem=d_send.at[r, k],
            recv_sem=d_recv.at[r, k],
            device_id=(mates[k], node),
            device_id_type=MESH,
        )

    def return_copy(r, k, part):
        some = pl.ds(k * cap + part * (cap // 2), cap // 2)
        return pltpu.make_async_remote_copy(
            src_ref=back.at[r, some],
            dst_ref=ret.at[r, some],
            send_sem=r_send.at[r, k, part],
            recv_sem=r_recv.at[r, k, part],
            device_id=(mates[k], node),
            device_id_type=MESH,
        )

    def z_copy(r, way, j):
        return pltpu.make_async_remote_copy(
            src_ref=shared.at[r, bit(j)],
            dst_ref=beside.at[r, way, bit(j)],
            send_sem=z_send.at[r, way, j],
            recv_sem=z_recv.at[r, way, j],
            device_id=(expert, way * down + (1 - way) * up),
            device_id_type=MESH,
        )

    def x_copy(r, j):
        return pltpu.make_async_remote_copy(
            src_ref=pair.at[r, bit(j)],
            dst_ref=across.at[r, bit(j)],
            send_sem=x_send.at[r, j],
            recv_sem=x_recv.at[r, j],
            device_id=(expert, facing),
            device_id_type=MESH,
        )

    def start_return(r, k):
        for part in range(2):
            return_copy(r, k, part).start()

    def slopes(r, half):
        part = pl.ds(half * rows, rows)
        pre = dot(got[r, part, :width], wide[...]) * factor
        grads = got[r, part, width:].astype(F32)
        slope[part, :] = (grads * 2.0 * jnp.maximum(pre, 0.0)).astype(BF16)

    def update_moment(r):
        total = jnp.zeros((1, hidden), F32)
        for j in range(CHUNKS):
            rung = pl.ds(j * tile, tile)
            grad = dot(got[r, :, rung], slope[...], 0, 0) * factor
            new = 0.9 * moment[rung, :] + grad
            moment[rung, :] = new
            total = total + jnp.sum(new * new, axis=0, keepdims=True)
        norm = jnp.sqrt(jnp.sum(total, axis=1, keepdims=True))
        scale = 1.0 / (norm + 1e-07)
        for j in range(CHUNKS):
            rung = pl.ds(j * tile, tile)
            orthog[rung, :] = (moment[rung, :] * scale).astype(BF16)

    def polynomial():
        part = hidden // 2
        for i in range(2):
            columns = pl.ds(i * part, part)
            gram[columns, :] = dot(orthog[:, columns], orthog[...], 0, 0).astype(BF16)
        for i in range(2):
            columns = pl.ds(i * part, part)
            own = gram[columns, :]
            square = dot(own, gram[...])
            poly[columns, :] = (-4.775 * own.astype(F32) + 2.0315 * square).astype(BF16)

    def applied(j):
        own = orthog[pl.ds(j * tile, tile), :]
        return (3.4445 * own.astype(F32) + dot(own, poly[...])).astype(BF16)

    def orthogonalize_and_share(r):
        def sweep(i, carry):
            polynomial()
            for j in range(CHUNKS):
                orthog[pl.ds(j * tile, tile), :] = applied(j)
            return carry

        lax.fori_loop(0, NS_STEPS - 1, sweep, 0)
        polynomial()
        for j in range(CHUNKS):
            rung = pl.ds(j * tile, tile)
            stepped = weight[rung, :] - step_size * applied(j).astype(F32)
            weight[rung, :] = stepped
            shared[r, rung, :] = stepped.astype(BF16)
            for i in range(PIECES // CHUNKS):
                z_copy(r, 0, j * (PIECES // CHUNKS) + i).start()
                z_copy(r, 1, j * (PIECES // CHUNKS) + i).start()

    def backward(r, k, blocks):
        part = pl.ds(k * cap, blocks * cap)
        for j in range(CHUNKS):
            rung = pl.ds(j * tile, tile)
            grad = dot(slope[part, :], wide[rung, :], 1, 1) * factor
            back[r, part, rung] = grad.astype(BF16)
        if k == 0:
            ret[r, fixed(0), :] = back[r, fixed(0), :]

    def unsort(r, k, blocks):
        for i in range(max(k, 1), k + blocks):
            return_copy(r, i, 0).wait_recv()
            return_copy(r, i, 1).wait_recv()
        part = pl.ds(k * cap, blocks * cap)

        for j in range(CHUNKS):
            columns = pl.ds(j * tile, tile)
            placed = dot(table[r, part, :], ret[r, part, columns], 0, 0)
            if k:
                placed = placed + ig[r, :, columns].astype(F32)
            ig[r, :, columns] = placed.astype(BF16)

    def pass_across(r, first, last):
        def body(j, carry):
            z_copy(r, 1 - odd, j).wait_recv()
            own = shared[r, bit(j), :].astype(F32)
            pair[r, bit(j), :] = (own + beside[r, 1 - odd, bit(j), :].astype(F32)).astype(BF16)
            x_copy(r, j).start()
            return carry

        lax.fori_loop(first, last, body, 0)

    def averaged(r, j):
        z_copy(r, odd, j).wait_recv()
        x_copy(r, j).wait_recv()
        neighbours = beside[r, 0, bit(j), :].astype(F32) + beside[r, 1, bit(j), :].astype(F32)
        neighbours = neighbours + across[r, bit(j), :].astype(F32)
        new = 0.4 * weight[bit(j), :] + 0.15 * neighbours
        weight[bit(j), :] = new
        return new

    load_route.wait()
    target = targets(0)
    loads[0].wait()
    loads[1].wait()
    for copy in (loads[2], loads[3], load_w, load_m):
        copy.start()
    choose(0, 2, target)
    pl.semaphore_wait(barrier, 3 + odd + 2 * odd_z)

    @pl.when(odd_z == 1)
    def _():
        for other in (up, down):
            pl.semaphore_signal(ready.at[0], inc=1, device_id=(expert, other), device_id_type=MESH)

    @pl.when(odd == 1)
    def _():
        pl.semaphore_signal(ready.at[1], inc=1, device_id=(expert, facing), device_id_type=MESH)

    dispatch_copy(0, 2).start()
    for k in (3, 1):
        choose(0, k, target)
        dispatch_copy(0, k).start()
    choose(0, 0, target)
    target = targets(1)
    loads[2].wait()
    loads[3].wait()
    for k in (2, 3, 1):
        choose(1, k, target)
        dispatch_copy(1, k).start()
    choose(1, 0, target)
    load_w.wait()

    def narrow(j, carry):
        wide[strip(j), :] = weight[strip(j), :].astype(BF16)
        return carry

    lax.fori_loop(0, CHUNKS, narrow, 0)
    load_m.wait()
    dispatch_copy(0, 1).wait_recv()
    slopes(0, 0)
    dispatch_copy(0, 2).wait_recv()
    dispatch_copy(0, 3).wait_recv()
    slopes(0, 1)
    update_moment(0)

    @pl.when(odd_z == 0)
    def _():
        pl.semaphore_wait(ready.at[0], 2)

    orthogonalize_and_share(0)
    backward(0, 2, 2)
    backward(0, 0, 2)

    @pl.when(odd == 0)
    def _():
        pl.semaphore_wait(ready.at[1], 1)

    pass_across(0, 0, PIECES)
    for k in (2, 3, 1):
        start_return(0, k)

    def mixed(j, carry):
        wide[bit(j), :] = averaged(0, j).astype(BF16)
        return carry

    lax.fori_loop(0, PIECES, mixed, 0)

    for k in (1, 2, 3):
        dispatch_copy(1, k).wait_recv()
    slopes(1, 0)
    slopes(1, 1)
    backward(1, 2, 2)
    start_return(1, 2)
    return_copy(1, 3, 0).start()
    update_moment(1)
    orthogonalize_and_share(1)
    backward(1, 0, 2)
    start_return(1, 1)
    pass_across(1, 0, PIECES // 2)
    unsort(0, 0, 4)
    pass_across(1, PIECES // 2, PIECES)
    return_copy(1, 3, 1).start()
    unsort(1, 0, 3)

    def finished(j, carry):
        averaged(1, j)
        return carry

    lax.fori_loop(0, PIECES, finished, 0)
    unsort(1, 3, 1)

    for r in range(ROUNDS):
        for k in (1, 2, 3):
            dispatch_copy(r, k).wait_send()
            return_copy(r, k, 0).wait_send()
            return_copy(r, k, 1).wait_send()

        def sent_all(j, carry, r=r):
            z_copy(r, 0, j).wait_send()
            z_copy(r, 1, j).wait_send()
            x_copy(r, j).wait_send()
            return carry

        lax.fori_loop(0, PIECES, sent_all, 0)


def store(weight, moment, ig, w_out, m_out, ig_out, sems):
    copies = (
        pltpu.make_async_copy(weight, w_out.at[0, 0], sems.at[0]),
        pltpu.make_async_copy(moment, m_out.at[0, 0], sems.at[1]),
        pltpu.make_async_copy(ig, ig_out, sems.at[2]),
    )
    for copy in copies:
        copy.start()
    for copy in copies:
        copy.wait()


def on_device(tokens, routing, out_grad, weights, momentum):
    rounds, rows, width = tokens.shape
    hidden = out_grad.shape[2]
    experts = weights.shape[1] * lax.axis_size("expert")
    nodes = lax.axis_size("node")
    slots = experts * (rows // 2)
    anywhere = pl.BlockSpec(memory_space=pl.ANY)
    in_hbm = pl.BlockSpec(memory_space=pltpu.HBM)
    on_chip = pl.BlockSpec(memory_space=pltpu.VMEM)
    dma = pltpu.SemaphoreType.DMA
    operands = (
        pltpu.with_memory_space_constraint(x, pltpu.HBM)
        for x in (tokens, routing, out_grad, weights, momentum)
    )
    weight, moment, in_grad = pl.pallas_call(
        functools.partial(kernel, nodes),
        name="muon_rounds",
        out_shape=(
            pltpu.VMEM((width, hidden), F32),
            pltpu.VMEM((width, hidden), F32),
            pltpu.VMEM((rounds, rows, width), BF16),
        ),
        in_specs=[in_hbm] * 5,
        out_specs=(on_chip, on_chip, on_chip),
        scratch_shapes=[
            pltpu.VMEM((rounds, rows), jnp.int32),
            pltpu.VMEM((rounds, rows, width), BF16),
            pltpu.VMEM((rounds, rows, hidden), BF16),
            pltpu.VMEM((width, hidden), BF16),
            pltpu.VMEM((rounds, slots, rows), BF16),
            pltpu.VMEM((rounds, slots, width + hidden), BF16),
            pltpu.VMEM((rounds, slots, width + hidden), BF16),
            pltpu.VMEM((slots, hidden), BF16),
            pltpu.VMEM((width, hidden), BF16),
            pltpu.VMEM((hidden, hidden), BF16),
            pltpu.VMEM((hidden, hidden), BF16),
            pltpu.VMEM((rounds, slots, width), BF16),
            pltpu.VMEM((rounds, slots, width), BF16),
            pltpu.VMEM((rounds, width, hidden), BF16),
            pltpu.VMEM((rounds, 2, width, hidden), BF16),
            pltpu.VMEM((rounds, width, hidden), BF16),
            pltpu.VMEM((rounds, width, hidden), BF16),
            dma((7,)),
            dma((rounds, 4)),
            dma((rounds, 4)),
            dma((rounds, 4, 2)),
            dma((rounds, 4, 2)),
            dma((rounds, 2, PIECES)),
            dma((rounds, 2, PIECES)),
            dma((rounds, PIECES)),
            dma((rounds, PIECES)),
            pltpu.SemaphoreType.REGULAR((2,)),
        ],
        compiler_params=pltpu.CompilerParams(
            collective_id=0, has_side_effects=True, vmem_limit_bytes=40 << 20
        ),
    )(*operands)
    return pl.pallas_call(
        store,
        name="store_results",
        out_shape=(
            jax.ShapeDtypeStruct(weights.shape, F32),
            jax.ShapeDtypeStruct(momentum.shape, F32),
            jax.ShapeDtypeStruct(tokens.shape, BF16),
        ),
        in_specs=[anywhere, anywhere, anywhere],
        out_specs=(anywhere, anywhere, anywhere),
        scratch_shapes=[dma((3,))],
        compiler_params=pltpu.CompilerParams(vmem_limit_bytes=1 << 20),
    )(weight, moment, in_grad)


def solution(mesh):
    return jax.shard_map(
        on_device,
        mesh=mesh,
        in_specs=(
            P(None, ("expert", "node"), None),
            P(None, ("expert", "node")),
            P(None, ("expert", "node"), None),
            P("node", "expert", None, None),
            P("node", "expert", None, None),
        ),
        out_specs=(
            P("node", "expert", None, None),
            P("node", "expert", None, None),
            P(None, ("expert", "node"), None),
        ),
        check_vma=False,
    )
```

```python
import functools
import math

import jax
import jax.numpy as jnp
from jax import lax
from jax.experimental import pallas as pl
from jax.experimental.pallas import tpu as pltpu
from jax.sharding import PartitionSpec as P

ROUNDS = 2
NS_STEPS = 3
CHUNKS = 4
PIECES = 16
DEPTH = 8
MESH = pl.DeviceIdType.MESH
F32 = jnp.float32
BF16 = jnp.bfloat16


def dot(a, b, ca=1, cb=0):
    return lax.dot_general(a, b, (((ca,), (cb,)), ((), ())), preferred_element_type=F32)


def kernel(
    nodes,
    tok_hbm, route_hbm, og_hbm, w_hbm, m_hbm,
    weight, moment, ig,
    route_ref, tok, og, wide, table, sent, got, slope, orthog, gram, poly,
    back, ret, shared, beside, pair, across,
    in_sem, d_send, d_recv, r_send, r_recv, z_send, z_recv, x_send, x_recv, ready,
):
    expert = lax.axis_index("expert")
    node = lax.axis_index("node")
    rows, width = tok.shape[1], tok.shape[2]
    hidden = og.shape[2]
    cap = rows // 2
    tile = width // CHUNKS
    piece = width // PIECES
    factor = 1.0 / math.sqrt(width)
    step_size = 0.1 * math.sqrt(width)

    chip, core = expert // 2, expert % 2
    mates = (
        expert,
        2 * chip + (1 - core),
        2 * (1 - chip) + core,
        2 * (1 - chip) + (1 - core),
    )
    odd = node % 2
    up = (node + 2) % nodes
    down = (node + nodes - 2) % nodes
    facing = node + 1 - 2 * odd

    loads = []
    for r in range(ROUNDS):
        loads.append(pltpu.make_async_copy(tok_hbm.at[r], tok.at[r], in_sem.at[2 * r]))
        loads.append(pltpu.make_async_copy(og_hbm.at[r], og.at[r], in_sem.at[2 * r + 1]))
    load_w = pltpu.make_async_copy(w_hbm.at[0, 0], weight, in_sem.at[4])
    load_route = pltpu.make_async_copy(route_hbm, route_ref, in_sem.at[6])
    load_m = pltpu.make_async_copy(m_hbm.at[0, 0], moment, in_sem.at[5])
    for copy in (load_route, *loads[:2]):
        copy.start()

    barrier = pltpu.get_barrier_semaphore()
    for mate in mates[1:]:
        pl.semaphore_signal(barrier, inc=1, device_id=(mate, node), device_id_type=MESH)

    def leads(other):
        z = (other // 2) % DEPTH
        return jnp.where((z == 0) | (z == 3), 1, 0)

    led_up = leads(up)
    led = leads(node)

    @pl.when(odd == 0)
    def _():
        pl.semaphore_signal(barrier, inc=1, device_id=(expert, facing), device_id_type=MESH)

    @pl.when(led_up == 0)
    def _():
        pl.semaphore_signal(barrier, inc=1, device_id=(expert, up), device_id_type=MESH)

    @pl.when(led == 1)
    def _():
        pl.semaphore_signal(barrier, inc=1, device_id=(expert, down), device_id_type=MESH)

    def fixed(index):
        return pl.ds(index * cap, cap)

    def strip(index):
        return pl.ds(pl.multiple_of(index * tile, tile), tile)

    def bit(index):
        return pl.ds(pl.multiple_of(index * piece, piece), piece)

    def targets(r):
        route = route_ref[r : r + 1, :]
        mask = lax.broadcasted_iota(jnp.int32, (16, rows), 0) == route
        first = lax.broadcasted_iota(jnp.int32, (rows, rows), 0)
        second = lax.broadcasted_iota(jnp.int32, (rows, rows), 1)
        earlier = jnp.where(first < second, 1.0, 0.0).astype(BF16)
        ranks = dot(jnp.where(mask, 1.0, 0.0).astype(BF16), earlier)
        rank = jnp.sum(jnp.where(mask, ranks, 0.0), axis=0, keepdims=True)
        return route.astype(F32) * float(cap) + rank

    def choose(r, k, target):
        slots = lax.broadcasted_iota(jnp.int32, (cap, rows), 0) + mates[k] * cap
        picks = jnp.where(slots.astype(F32) == target, 1.0, 0.0).astype(BF16)
        table[r, fixed(k), :] = picks
        held = sent if k else got
        held[r, fixed(k), :width] = dot(picks, tok[r]).astype(BF16)
        held[r, fixed(k), width:] = dot(picks, og[r]).astype(BF16)

    def dispatch_copy(r, k):
        return pltpu.make_async_remote_copy(
            src_ref=sent.at[r, fixed(k)],
            dst_ref=got.at[r, fixed(k)],
            send_sem=d_send.at[r, k],
            recv_sem=d_recv.at[r, k],
            device_id=(mates[k], node),
            device_id_type=MESH,
        )

    def return_copy(r, k, part):
        some = pl.ds(k * cap + part * (cap // 2), cap // 2)
        return pltpu.make_async_remote_copy(
            src_ref=back.at[r, some],
            dst_ref=ret.at[r, some],
            send_sem=r_send.at[r, k, part],
            recv_sem=r_recv.at[r, k, part],
            device_id=(mates[k], node),
            device_id_type=MESH,
        )

    def z_copy(r, way, j):
        return pltpu.make_async_remote_copy(
            src_ref=shared.at[r, bit(j)],
            dst_ref=beside.at[r, way, bit(j)],
            send_sem=z_send.at[r, way, j],
            recv_sem=z_recv.at[r, way, j],
            device_id=(expert, way * down + (1 - way) * up),
            device_id_type=MESH,
        )

    def x_copy(r, j):
        return pltpu.make_async_remote_copy(
            src_ref=pair.at[r, bit(j)],
            dst_ref=across.at[r, bit(j)],
            send_sem=x_send.at[r, j],
            recv_sem=x_recv.at[r, j],
            device_id=(expert, facing),
            device_id_type=MESH,
        )

    def start_return(r, k):
        for part in range(2):
            return_copy(r, k, part).start()

    def slopes(r, half):
        part = pl.ds(half * rows, rows)
        pre = dot(got[r, part, :width], wide[...]) * factor
        grads = got[r, part, width:].astype(F32)
        slope[part, :] = (grads * 2.0 * jnp.maximum(pre, 0.0)).astype(BF16)

    def update_moment(r):
        total = jnp.zeros((1, hidden), F32)
        for j in range(CHUNKS):
            rung = pl.ds(j * tile, tile)
            grad = dot(got[r, :, rung], slope[...], 0, 0) * factor
            new = 0.9 * moment[rung, :] + grad
            moment[rung, :] = new
            total = total + jnp.sum(new * new, axis=0, keepdims=True)
        norm = jnp.sqrt(jnp.sum(total, axis=1, keepdims=True))
        scale = 1.0 / (norm + 1e-07)
        for j in range(CHUNKS):
            rung = pl.ds(j * tile, tile)
            orthog[rung, :] = (moment[rung, :] * scale).astype(BF16)

    def polynomial():
        part = hidden // 2
        for i in range(2):
            columns = pl.ds(i * part, part)
            gram[columns, :] = dot(orthog[:, columns], orthog[...], 0, 0).astype(BF16)
        for i in range(2):
            columns = pl.ds(i * part, part)
            own = gram[columns, :]
            square = dot(own, gram[...])
            poly[columns, :] = (-4.775 * own.astype(F32) + 2.0315 * square).astype(BF16)

    def applied(j):
        own = orthog[pl.ds(j * tile, tile), :]
        return (3.4445 * own.astype(F32) + dot(own, poly[...])).astype(BF16)

    def orthogonalize_and_share(r):
        def sweep(i, carry):
            polynomial()
            for j in range(CHUNKS):
                orthog[pl.ds(j * tile, tile), :] = applied(j)
            return carry

        lax.fori_loop(0, NS_STEPS - 1, sweep, 0)
        polynomial()
        for j in range(CHUNKS):
            rung = pl.ds(j * tile, tile)
            stepped = weight[rung, :] - step_size * applied(j).astype(F32)
            weight[rung, :] = stepped
            shared[r, rung, :] = stepped.astype(BF16)
            for i in range(PIECES // CHUNKS):
                z_copy(r, 0, j * (PIECES // CHUNKS) + i).start()
                z_copy(r, 1, j * (PIECES // CHUNKS) + i).start()

    def backward(r, k, blocks):
        part = pl.ds(k * cap, blocks * cap)
        for j in range(CHUNKS):
            rung = pl.ds(j * tile, tile)
            grad = dot(slope[part, :], wide[rung, :], 1, 1) * factor
            back[r, part, rung] = grad.astype(BF16)
        if k == 0:
            ret[r, fixed(0), :] = back[r, fixed(0), :]

    def unsort(r, k, blocks):
        for i in range(max(k, 1), k + blocks):
            return_copy(r, i, 0).wait_recv()
            return_copy(r, i, 1).wait_recv()
        part = pl.ds(k * cap, blocks * cap)

        for j in range(CHUNKS):
            columns = pl.ds(j * tile, tile)
            placed = dot(table[r, part, :], ret[r, part, columns], 0, 0)
            if k:
                placed = placed + ig[r, :, columns].astype(F32)
            ig[r, :, columns] = placed.astype(BF16)

    def pass_across(r, first, last):
        def body(j, carry):
            z_copy(r, 1 - odd, j).wait_recv()
            own = shared[r, bit(j), :].astype(F32)
            pair[r, bit(j), :] = (own + beside[r, 1 - odd, bit(j), :].astype(F32)).astype(BF16)
            x_copy(r, j).start()
            return carry

        lax.fori_loop(first, last, body, 0)

    def averaged(r, j):
        z_copy(r, odd, j).wait_recv()
        x_copy(r, j).wait_recv()
        neighbours = beside[r, 0, bit(j), :].astype(F32) + beside[r, 1, bit(j), :].astype(F32)
        neighbours = neighbours + across[r, bit(j), :].astype(F32)
        new = 0.4 * weight[bit(j), :] + 0.15 * neighbours
        weight[bit(j), :] = new
        return new

    load_route.wait()
    target = targets(0)
    loads[0].wait()
    loads[1].wait()
    for copy in (loads[2], loads[3], load_w, load_m):
        copy.start()
    choose(0, 2, target)
    pl.semaphore_wait(barrier, 3 + odd + led_up + (1 - led))

    @pl.when(led_up == 1)
    def _():
        pl.semaphore_signal(ready.at[0], inc=1, device_id=(expert, up), device_id_type=MESH)

    @pl.when(led == 0)
    def _():
        pl.semaphore_signal(ready.at[2], inc=1, device_id=(expert, down), device_id_type=MESH)

    @pl.when(odd == 1)
    def _():
        pl.semaphore_signal(ready.at[1], inc=1, device_id=(expert, facing), device_id_type=MESH)

    dispatch_copy(0, 2).start()
    for k in (3, 1):
        choose(0, k, target)
        dispatch_copy(0, k).start()
    choose(0, 0, target)
    target = targets(1)
    loads[2].wait()
    loads[3].wait()
    for k in (2, 3, 1):
        choose(1, k, target)
        dispatch_copy(1, k).start()
    choose(1, 0, target)
    load_w.wait()

    def narrow(j, carry):
        wide[strip(j), :] = weight[strip(j), :].astype(BF16)
        return carry

    lax.fori_loop(0, CHUNKS, narrow, 0)
    load_m.wait()
    dispatch_copy(0, 1).wait_recv()
    slopes(0, 0)
    dispatch_copy(0, 2).wait_recv()
    dispatch_copy(0, 3).wait_recv()
    slopes(0, 1)
    update_moment(0)

    @pl.when(led == 1)
    def _():
        pl.semaphore_wait(ready.at[0], 1)

    @pl.when(led_up == 0)
    def _():
        pl.semaphore_wait(ready.at[2], 1)

    orthogonalize_and_share(0)
    backward(0, 2, 2)
    backward(0, 0, 2)

    @pl.when(odd == 0)
    def _():
        pl.semaphore_wait(ready.at[1], 1)

    pass_across(0, 0, PIECES)
    for k in (2, 3, 1):
        start_return(0, k)

    def mixed(j, carry):
        wide[bit(j), :] = averaged(0, j).astype(BF16)
        return carry

    lax.fori_loop(0, PIECES, mixed, 0)

    for k in (1, 2, 3):
        dispatch_copy(1, k).wait_recv()
    slopes(1, 0)
    slopes(1, 1)
    backward(1, 2, 1)
    start_return(1, 2)
    update_moment(1)
    orthogonalize_and_share(1)
    backward(1, 3, 1)
    return_copy(1, 3, 0).start()
    backward(1, 0, 2)
    start_return(1, 1)
    pass_across(1, 0, PIECES // 2)
    unsort(0, 0, 4)
    pass_across(1, PIECES // 2, PIECES)
    return_copy(1, 3, 1).start()
    unsort(1, 0, 3)

    def finished(j, carry):
        averaged(1, j)
        return carry

    lax.fori_loop(0, PIECES, finished, 0)
    unsort(1, 3, 1)

    for r in range(ROUNDS):
        for k in (1, 2, 3):
            dispatch_copy(r, k).wait_send()
            return_copy(r, k, 0).wait_send()
            return_copy(r, k, 1).wait_send()

        def sent_all(j, carry, r=r):
            z_copy(r, 0, j).wait_send()
            z_copy(r, 1, j).wait_send()
            x_copy(r, j).wait_send()
            return carry

        lax.fori_loop(0, PIECES, sent_all, 0)


def store(weight, moment, ig, w_out, m_out, ig_out, sems):
    copies = (
        pltpu.make_async_copy(weight, w_out.at[0, 0], sems.at[0]),
        pltpu.make_async_copy(moment, m_out.at[0, 0], sems.at[1]),
        pltpu.make_async_copy(ig, ig_out, sems.at[2]),
    )
    for copy in copies:
        copy.start()
    for copy in copies:
        copy.wait()


def on_device(tokens, routing, out_grad, weights, momentum):
    rounds, rows, width = tokens.shape
    hidden = out_grad.shape[2]
    experts = weights.shape[1] * lax.axis_size("expert")
    nodes = lax.axis_size("node")
    slots = experts * (rows // 2)
    anywhere = pl.BlockSpec(memory_space=pl.ANY)
    in_hbm = pl.BlockSpec(memory_space=pltpu.HBM)
    on_chip = pl.BlockSpec(memory_space=pltpu.VMEM)
    dma = pltpu.SemaphoreType.DMA
    operands = (
        pltpu.with_memory_space_constraint(x, pltpu.HBM)
        for x in (tokens, routing, out_grad, weights, momentum)
    )
    weight, moment, in_grad = pl.pallas_call(
        functools.partial(kernel, nodes),
        name="muon_rounds",
        out_shape=(
            pltpu.VMEM((width, hidden), F32),
            pltpu.VMEM((width, hidden), F32),
            pltpu.VMEM((rounds, rows, width), BF16),
        ),
        in_specs=[in_hbm] * 5,
        out_specs=(on_chip, on_chip, on_chip),
        scratch_shapes=[
            pltpu.VMEM((rounds, rows), jnp.int32),
            pltpu.VMEM((rounds, rows, width), BF16),
            pltpu.VMEM((rounds, rows, hidden), BF16),
            pltpu.VMEM((width, hidden), BF16),
            pltpu.VMEM((rounds, slots, rows), BF16),
            pltpu.VMEM((rounds, slots, width + hidden), BF16),
            pltpu.VMEM((rounds, slots, width + hidden), BF16),
            pltpu.VMEM((slots, hidden), BF16),
            pltpu.VMEM((width, hidden), BF16),
            pltpu.VMEM((hidden, hidden), BF16),
            pltpu.VMEM((hidden, hidden), BF16),
            pltpu.VMEM((rounds, slots, width), BF16),
            pltpu.VMEM((rounds, slots, width), BF16),
            pltpu.VMEM((rounds, width, hidden), BF16),
            pltpu.VMEM((rounds, 2, width, hidden), BF16),
            pltpu.VMEM((rounds, width, hidden), BF16),
            pltpu.VMEM((rounds, width, hidden), BF16),
            dma((7,)),
            dma((rounds, 4)),
            dma((rounds, 4)),
            dma((rounds, 4, 2)),
            dma((rounds, 4, 2)),
            dma((rounds, 2, PIECES)),
            dma((rounds, 2, PIECES)),
            dma((rounds, PIECES)),
            dma((rounds, PIECES)),
            pltpu.SemaphoreType.REGULAR((3,)),
        ],
        compiler_params=pltpu.CompilerParams(
            collective_id=0, has_side_effects=True, vmem_limit_bytes=40 << 20
        ),
    )(*operands)
    return pl.pallas_call(
        store,
        name="store_results",
        out_shape=(
            jax.ShapeDtypeStruct(weights.shape, F32),
            jax.ShapeDtypeStruct(momentum.shape, F32),
            jax.ShapeDtypeStruct(tokens.shape, BF16),
        ),
        in_specs=[anywhere, anywhere, anywhere],
        out_specs=(anywhere, anywhere, anywhere),
        scratch_shapes=[dma((3,))],
        compiler_params=pltpu.CompilerParams(vmem_limit_bytes=1 << 20),
    )(weight, moment, in_grad)


def solution(mesh):
    return jax.shard_map(
        on_device,
        mesh=mesh,
        in_specs=(
            P(None, ("expert", "node"), None),
            P(None, ("expert", "node")),
            P(None, ("expert", "node"), None),
            P("node", "expert", None, None),
            P("node", "expert", None, None),
        ),
        out_specs=(
            P("node", "expert", None, None),
            P("node", "expert", None, None),
            P(None, ("expert", "node"), None),
        ),
        check_vma=False,
    )
```

```python
import functools
import math

import jax
import jax.numpy as jnp
from jax import lax
from jax.experimental import pallas as pl
from jax.experimental.pallas import tpu as pltpu
from jax.sharding import PartitionSpec as P

ROUNDS = 2
NS_STEPS = 3
CHUNKS = 4
PIECES = 8
EARLY = 2
DEPTH = 8
MESH = pl.DeviceIdType.MESH
F32 = jnp.float32
BF16 = jnp.bfloat16


def dot(a, b, ca=1, cb=0):
    return lax.dot_general(a, b, (((ca,), (cb,)), ((), ())), preferred_element_type=F32)


def kernel(
    nodes,
    tok_hbm, route_hbm, og_hbm, w_hbm, m_hbm,
    weight, moment, ig,
    route_ref, tok, og, wide, table, sent, got, slope, orthog, gram, poly,
    back, ret, shared, beside, pair, across,
    in_sem, d_send, d_recv, r_send, r_recv, z_send, z_recv, x_send, x_recv, ready,
):
    expert = lax.axis_index("expert")
    node = lax.axis_index("node")
    rows, width = tok.shape[1], tok.shape[2]
    hidden = og.shape[2]
    cap = rows // 2
    tile = width // CHUNKS
    piece = width // PIECES
    factor = 1.0 / math.sqrt(width)
    step_size = 0.1 * math.sqrt(width)

    chip, core = expert // 2, expert % 2
    mates = (
        expert,
        2 * chip + (1 - core),
        2 * (1 - chip) + core,
        2 * (1 - chip) + (1 - core),
    )
    odd = node % 2
    up = (node + 2) % nodes
    down = (node + nodes - 2) % nodes
    facing = node + 1 - 2 * odd

    loads = []
    for r in range(ROUNDS):
        loads.append(pltpu.make_async_copy(tok_hbm.at[r], tok.at[r], in_sem.at[2 * r]))
        loads.append(pltpu.make_async_copy(og_hbm.at[r], og.at[r], in_sem.at[2 * r + 1]))
    load_w = pltpu.make_async_copy(w_hbm.at[0, 0], weight, in_sem.at[4])
    load_route = pltpu.make_async_copy(route_hbm, route_ref, in_sem.at[6])
    load_m = pltpu.make_async_copy(m_hbm.at[0, 0], moment, in_sem.at[5])
    for copy in (load_route, *loads[:2]):
        copy.start()

    barrier = pltpu.get_barrier_semaphore()
    for mate in mates[1:]:
        pl.semaphore_signal(barrier, inc=1, device_id=(mate, node), device_id_type=MESH)

    def leads(other):
        z = (other // 2) % DEPTH
        return jnp.where((z == 0) | (z == 3), 1, 0)

    led_up = leads(up)
    led = leads(node)

    @pl.when(odd == 0)
    def _():
        pl.semaphore_signal(barrier, inc=1, device_id=(expert, facing), device_id_type=MESH)

    @pl.when(led_up == 0)
    def _():
        pl.semaphore_signal(barrier, inc=1, device_id=(expert, up), device_id_type=MESH)

    @pl.when(led == 1)
    def _():
        pl.semaphore_signal(barrier, inc=1, device_id=(expert, down), device_id_type=MESH)

    def fixed(index):
        return pl.ds(index * cap, cap)

    def strip(index):
        return pl.ds(pl.multiple_of(index * tile, tile), tile)

    def bit(index):
        return pl.ds(pl.multiple_of(index * piece, piece), piece)

    def targets(r):
        route = route_ref[r : r + 1, :]
        mask = lax.broadcasted_iota(jnp.int32, (16, rows), 0) == route
        first = lax.broadcasted_iota(jnp.int32, (rows, rows), 0)
        second = lax.broadcasted_iota(jnp.int32, (rows, rows), 1)
        earlier = jnp.where(first < second, 1.0, 0.0).astype(BF16)
        ranks = dot(jnp.where(mask, 1.0, 0.0).astype(BF16), earlier)
        rank = jnp.sum(jnp.where(mask, ranks, 0.0), axis=0, keepdims=True)
        return route.astype(F32) * float(cap) + rank

    def choose(r, k, target):
        slots = lax.broadcasted_iota(jnp.int32, (cap, rows), 0) + mates[k] * cap
        picks = jnp.where(slots.astype(F32) == target, 1.0, 0.0).astype(BF16)
        table[r, fixed(k), :] = picks
        held = sent if k else got
        held[r, fixed(k), :width] = dot(picks, tok[r]).astype(BF16)
        held[r, fixed(k), width:] = dot(picks, og[r]).astype(BF16)

    def dispatch_copy(r, k):
        return pltpu.make_async_remote_copy(
            src_ref=sent.at[r, fixed(k)],
            dst_ref=got.at[r, fixed(k)],
            send_sem=d_send.at[r, k],
            recv_sem=d_recv.at[r, k],
            device_id=(mates[k], node),
            device_id_type=MESH,
        )

    def return_copy(r, k, part):
        some = pl.ds(k * cap + part * (cap // 2), cap // 2)
        return pltpu.make_async_remote_copy(
            src_ref=back.at[r, some],
            dst_ref=ret.at[r, some],
            send_sem=r_send.at[r, k, part],
            recv_sem=r_recv.at[r, k, part],
            device_id=(mates[k], node),
            device_id_type=MESH,
        )

    def z_copy(r, way, j, held=shared):
        return pltpu.make_async_remote_copy(
            src_ref=held.at[r, bit(j)],
            dst_ref=beside.at[r, way, bit(j)],
            send_sem=z_send.at[r, way, j],
            recv_sem=z_recv.at[r, way, j],
            device_id=(expert, way * down + (1 - way) * up),
            device_id_type=MESH,
        )

    def x_copy(r, j, held=pair):
        return pltpu.make_async_remote_copy(
            src_ref=held.at[r, bit(j)],
            dst_ref=across.at[r, bit(j)],
            send_sem=x_send.at[r, j],
            recv_sem=x_recv.at[r, j],
            device_id=(expert, facing),
            device_id_type=MESH,
        )

    def start_return(r, k):
        for part in range(2):
            return_copy(r, k, part).start()

    def slopes(r, half):
        part = pl.ds(half * rows, rows)
        pre = dot(got[r, part, :width], wide[...]) * factor
        grads = got[r, part, width:].astype(F32)
        slope[part, :] = (grads * 2.0 * jnp.maximum(pre, 0.0)).astype(BF16)

    def update_moment(r):
        total = jnp.zeros((1, hidden), F32)
        for j in range(CHUNKS):
            rung = pl.ds(j * tile, tile)
            grad = dot(got[r, :, rung], slope[...], 0, 0) * factor
            new = 0.9 * moment[rung, :] + grad
            moment[rung, :] = new
            total = total + jnp.sum(new * new, axis=0, keepdims=True)
        norm = jnp.sqrt(jnp.sum(total, axis=1, keepdims=True))
        scale = 1.0 / (norm + 1e-07)
        for j in range(CHUNKS):
            rung = pl.ds(j * tile, tile)
            orthog[rung, :] = (moment[rung, :] * scale).astype(BF16)

    def polynomial():
        part = hidden // 2
        for i in range(2):
            columns = pl.ds(i * part, part)
            gram[columns, :] = dot(orthog[:, columns], orthog[...], 0, 0).astype(BF16)
        for i in range(2):
            columns = pl.ds(i * part, part)
            own = gram[columns, :]
            square = dot(own, gram[...])
            poly[columns, :] = (-4.775 * own.astype(F32) + 2.0315 * square).astype(BF16)

    def applied(j):
        own = orthog[pl.ds(j * tile, tile), :]
        return (3.4445 * own.astype(F32) + dot(own, poly[...])).astype(BF16)

    def orthogonalize_and_share(r):
        def sweep(i, carry):
            polynomial()
            for j in range(CHUNKS):
                orthog[pl.ds(j * tile, tile), :] = applied(j)
            return carry

        lax.fori_loop(0, NS_STEPS - 1, sweep, 0)
        polynomial()
        for j in range(CHUNKS):
            rung = pl.ds(j * tile, tile)
            stepped = weight[rung, :] - step_size * applied(j).astype(F32)
            weight[rung, :] = stepped
            shared[r, rung, :] = stepped.astype(BF16)
            for i in range(j * (PIECES // CHUNKS), (j + 1) * (PIECES // CHUNKS)):
                if i < EARLY:
                    x_copy(r, i, shared).start()
                else:
                    z_copy(r, 0, i).start()
                    z_copy(r, 1, i).start()

    def backward(r, k, blocks):
        part = pl.ds(k * cap, blocks * cap)
        for j in range(CHUNKS):
            rung = pl.ds(j * tile, tile)
            grad = dot(slope[part, :], wide[rung, :], 1, 1) * factor
            back[r, part, rung] = grad.astype(BF16)
        if k == 0:
            ret[r, fixed(0), :] = back[r, fixed(0), :]

    def unsort(r, k, blocks):
        for i in range(max(k, 1), k + blocks):
            return_copy(r, i, 0).wait_recv()
            return_copy(r, i, 1).wait_recv()
        part = pl.ds(k * cap, blocks * cap)

        for j in range(CHUNKS):
            columns = pl.ds(j * tile, tile)
            placed = dot(table[r, part, :], ret[r, part, columns], 0, 0)
            if k:
                placed = placed + ig[r, :, columns].astype(F32)
            ig[r, :, columns] = placed.astype(BF16)

    def pass_across(r, first, last):
        def body(j, carry):
            z_copy(r, 1 - odd, j).wait_recv()
            own = shared[r, bit(j), :].astype(F32)
            pair[r, bit(j), :] = (own + beside[r, 1 - odd, bit(j), :].astype(F32)).astype(BF16)
            x_copy(r, j).start()
            return carry

        lax.fori_loop(first, last, body, 0)

    def pass_along(r):
        for j in range(EARLY):
            z_copy(r, 1 - odd, j).start()
            x_copy(r, j, shared).wait_recv()
            own = shared[r, bit(j), :].astype(F32)
            pair[r, bit(j), :] = (own + across[r, bit(j), :].astype(F32)).astype(BF16)
            z_copy(r, odd, j, pair).start()

    def averaged(r, j):
        neighbours = beside[r, 0, bit(j), :].astype(F32) + beside[r, 1, bit(j), :].astype(F32)
        neighbours = neighbours + across[r, bit(j), :].astype(F32)
        new = 0.4 * weight[bit(j), :] + 0.15 * neighbours
        weight[bit(j), :] = new
        return new

    def averages(r, use):
        for j in range(EARLY):
            z_copy(r, 0, j).wait_recv()
            z_copy(r, 1, j).wait_recv()
            use(j, averaged(r, j))

        def body(j, carry):
            z_copy(r, odd, j).wait_recv()
            x_copy(r, j).wait_recv()
            use(j, averaged(r, j))
            return carry

        lax.fori_loop(EARLY, PIECES, body, 0)

    load_route.wait()
    target = targets(0)
    loads[0].wait()
    loads[1].wait()
    for copy in (loads[2], loads[3], load_w, load_m):
        copy.start()
    choose(0, 2, target)
    pl.semaphore_wait(barrier, 3 + odd + led_up + (1 - led))

    @pl.when(led_up == 1)
    def _():
        pl.semaphore_signal(ready.at[0], inc=1, device_id=(expert, up), device_id_type=MESH)

    @pl.when(led == 0)
    def _():
        pl.semaphore_signal(ready.at[2], inc=1, device_id=(expert, down), device_id_type=MESH)

    @pl.when(odd == 1)
    def _():
        pl.semaphore_signal(ready.at[1], inc=1, device_id=(expert, facing), device_id_type=MESH)

    dispatch_copy(0, 2).start()
    for k in (3, 1):
        choose(0, k, target)
        dispatch_copy(0, k).start()
    choose(0, 0, target)
    target = targets(1)
    loads[2].wait()
    loads[3].wait()
    for k in (2, 3, 1):
        choose(1, k, target)
        dispatch_copy(1, k).start()
    choose(1, 0, target)
    load_w.wait()

    def narrow(j, carry):
        wide[strip(j), :] = weight[strip(j), :].astype(BF16)
        return carry

    lax.fori_loop(0, CHUNKS, narrow, 0)
    load_m.wait()
    dispatch_copy(0, 1).wait_recv()
    slopes(0, 0)
    dispatch_copy(0, 2).wait_recv()
    dispatch_copy(0, 3).wait_recv()
    slopes(0, 1)
    update_moment(0)

    @pl.when(led == 1)
    def _():
        pl.semaphore_wait(ready.at[0], 1)

    @pl.when(led_up == 0)
    def _():
        pl.semaphore_wait(ready.at[2], 1)

    @pl.when(odd == 0)
    def _():
        pl.semaphore_wait(ready.at[1], 1)

    orthogonalize_and_share(0)
    backward(0, 2, 2)
    backward(0, 0, 2)
    pass_across(0, EARLY, PIECES)
    for k in (2, 3, 1):
        start_return(0, k)
    pass_along(0)

    def narrowed(j, new):
        wide[bit(j), :] = new.astype(BF16)

    averages(0, narrowed)

    for k in (1, 2, 3):
        dispatch_copy(1, k).wait_recv()
    slopes(1, 0)
    slopes(1, 1)
    backward(1, 2, 1)
    start_return(1, 2)
    update_moment(1)
    orthogonalize_and_share(1)
    backward(1, 3, 1)
    return_copy(1, 3, 0).start()
    backward(1, 0, 2)
    start_return(1, 1)
    pass_across(1, EARLY, PIECES // 2)
    unsort(0, 0, 4)
    pass_across(1, PIECES // 2, PIECES)
    return_copy(1, 3, 1).start()
    pass_along(1)
    unsort(1, 0, 3)
    averages(1, lambda j, new: None)
    unsort(1, 3, 1)

    for r in range(ROUNDS):
        for k in (1, 2, 3):
            dispatch_copy(r, k).wait_send()
            return_copy(r, k, 0).wait_send()
            return_copy(r, k, 1).wait_send()

        def sent_all(j, carry, r=r):
            z_copy(r, 0, j).wait_send()
            z_copy(r, 1, j).wait_send()
            x_copy(r, j).wait_send()
            return carry

        lax.fori_loop(0, PIECES, sent_all, 0)


def store(weight, moment, ig, w_out, m_out, ig_out, sems):
    copies = (
        pltpu.make_async_copy(weight, w_out.at[0, 0], sems.at[0]),
        pltpu.make_async_copy(moment, m_out.at[0, 0], sems.at[1]),
        pltpu.make_async_copy(ig, ig_out, sems.at[2]),
    )
    for copy in copies:
        copy.start()
    for copy in copies:
        copy.wait()


def on_device(tokens, routing, out_grad, weights, momentum):
    rounds, rows, width = tokens.shape
    hidden = out_grad.shape[2]
    experts = weights.shape[1] * lax.axis_size("expert")
    nodes = lax.axis_size("node")
    slots = experts * (rows // 2)
    anywhere = pl.BlockSpec(memory_space=pl.ANY)
    in_hbm = pl.BlockSpec(memory_space=pltpu.HBM)
    on_chip = pl.BlockSpec(memory_space=pltpu.VMEM)
    dma = pltpu.SemaphoreType.DMA
    operands = (
        pltpu.with_memory_space_constraint(x, pltpu.HBM)
        for x in (tokens, routing, out_grad, weights, momentum)
    )
    weight, moment, in_grad = pl.pallas_call(
        functools.partial(kernel, nodes),
        name="muon_rounds",
        out_shape=(
            pltpu.VMEM((width, hidden), F32),
            pltpu.VMEM((width, hidden), F32),
            pltpu.VMEM((rounds, rows, width), BF16),
        ),
        in_specs=[in_hbm] * 5,
        out_specs=(on_chip, on_chip, on_chip),
        scratch_shapes=[
            pltpu.VMEM((rounds, rows), jnp.int32),
            pltpu.VMEM((rounds, rows, width), BF16),
            pltpu.VMEM((rounds, rows, hidden), BF16),
            pltpu.VMEM((width, hidden), BF16),
            pltpu.VMEM((rounds, slots, rows), BF16),
            pltpu.VMEM((rounds, slots, width + hidden), BF16),
            pltpu.VMEM((rounds, slots, width + hidden), BF16),
            pltpu.VMEM((slots, hidden), BF16),
            pltpu.VMEM((width, hidden), BF16),
            pltpu.VMEM((hidden, hidden), BF16),
            pltpu.VMEM((hidden, hidden), BF16),
            pltpu.VMEM((rounds, slots, width), BF16),
            pltpu.VMEM((rounds, slots, width), BF16),
            pltpu.VMEM((rounds, width, hidden), BF16),
            pltpu.VMEM((rounds, 2, width, hidden), BF16),
            pltpu.VMEM((rounds, width, hidden), BF16),
            pltpu.VMEM((rounds, width, hidden), BF16),
            dma((7,)),
            dma((rounds, 4)),
            dma((rounds, 4)),
            dma((rounds, 4, 2)),
            dma((rounds, 4, 2)),
            dma((rounds, 2, PIECES)),
            dma((rounds, 2, PIECES)),
            dma((rounds, PIECES)),
            dma((rounds, PIECES)),
            pltpu.SemaphoreType.REGULAR((3,)),
        ],
        compiler_params=pltpu.CompilerParams(
            collective_id=0, has_side_effects=True, vmem_limit_bytes=40 << 20
        ),
    )(*operands)
    return pl.pallas_call(
        store,
        name="store_results",
        out_shape=(
            jax.ShapeDtypeStruct(weights.shape, F32),
            jax.ShapeDtypeStruct(momentum.shape, F32),
            jax.ShapeDtypeStruct(tokens.shape, BF16),
        ),
        in_specs=[anywhere, anywhere, anywhere],
        out_specs=(anywhere, anywhere, anywhere),
        scratch_shapes=[dma((3,))],
        compiler_params=pltpu.CompilerParams(vmem_limit_bytes=1 << 20),
    )(weight, moment, in_grad)


def solution(mesh):
    return jax.shard_map(
        on_device,
        mesh=mesh,
        in_specs=(
            P(None, ("expert", "node"), None),
            P(None, ("expert", "node")),
            P(None, ("expert", "node"), None),
            P("node", "expert", None, None),
            P("node", "expert", None, None),
        ),
        out_specs=(
            P("node", "expert", None, None),
            P("node", "expert", None, None),
            P(None, ("expert", "node"), None),
        ),
        check_vma=False,
    )
```

```python
import functools
import math

import jax
import jax.numpy as jnp
from jax import lax
from jax.experimental import pallas as pl
from jax.experimental.pallas import tpu as pltpu
from jax.sharding import PartitionSpec as P

ROUNDS = 2
NS_STEPS = 3
CHUNKS = 4
PIECES = 4
EARLY = 1
DEPTH = 8
MESH = pl.DeviceIdType.MESH
F32 = jnp.float32
BF16 = jnp.bfloat16


def dot(a, b, ca=1, cb=0):
    return lax.dot_general(a, b, (((ca,), (cb,)), ((), ())), preferred_element_type=F32)


def kernel(
    nodes,
    tok_hbm, route_hbm, og_hbm, w_hbm, m_hbm,
    weight, moment, ig,
    route_ref, tok, og, wide, table, sent, got, slope, orthog, gram, poly,
    back, ret, shared, beside, pair, across,
    in_sem, d_send, d_recv, r_send, r_recv, z_send, z_recv, x_send, x_recv, ready,
):
    expert = lax.axis_index("expert")
    node = lax.axis_index("node")
    rows, width = tok.shape[1], tok.shape[2]
    hidden = og.shape[2]
    cap = rows // 2
    tile = width // CHUNKS
    piece = width // PIECES
    factor = 1.0 / math.sqrt(width)
    step_size = 0.1 * math.sqrt(width)

    chip, core = expert // 2, expert % 2
    mates = (
        expert,
        2 * chip + (1 - core),
        2 * (1 - chip) + core,
        2 * (1 - chip) + (1 - core),
    )
    odd = node % 2
    up = (node + 2) % nodes
    down = (node + nodes - 2) % nodes
    facing = node + 1 - 2 * odd

    loads = []
    for r in range(ROUNDS):
        loads.append(pltpu.make_async_copy(tok_hbm.at[r], tok.at[r], in_sem.at[2 * r]))
        loads.append(pltpu.make_async_copy(og_hbm.at[r], og.at[r], in_sem.at[2 * r + 1]))
    load_w = pltpu.make_async_copy(w_hbm.at[0, 0], weight, in_sem.at[4])
    load_route = pltpu.make_async_copy(route_hbm, route_ref, in_sem.at[6])
    load_m = pltpu.make_async_copy(m_hbm.at[0, 0], moment, in_sem.at[5])
    for copy in (load_route, *loads[:2]):
        copy.start()

    barrier = pltpu.get_barrier_semaphore()
    for mate in mates[1:]:
        pl.semaphore_signal(barrier, inc=1, device_id=(mate, node), device_id_type=MESH)

    def leads(other):
        z = (other // 2) % DEPTH
        return jnp.where((z == 0) | (z == 3), 1, 0)

    led_up = leads(up)
    led = leads(node)

    @pl.when(odd == 0)
    def _():
        pl.semaphore_signal(barrier, inc=1, device_id=(expert, facing), device_id_type=MESH)

    @pl.when(led_up == 0)
    def _():
        pl.semaphore_signal(barrier, inc=1, device_id=(expert, up), device_id_type=MESH)

    @pl.when(led == 1)
    def _():
        pl.semaphore_signal(barrier, inc=1, device_id=(expert, down), device_id_type=MESH)

    def fixed(index):
        return pl.ds(index * cap, cap)

    def strip(index):
        return pl.ds(pl.multiple_of(index * tile, tile), tile)

    def bit(index):
        return pl.ds(pl.multiple_of(index * piece, piece), piece)

    def targets(r):
        route = route_ref[r : r + 1, :]
        mask = lax.broadcasted_iota(jnp.int32, (16, rows), 0) == route
        first = lax.broadcasted_iota(jnp.int32, (rows, rows), 0)
        second = lax.broadcasted_iota(jnp.int32, (rows, rows), 1)
        earlier = jnp.where(first < second, 1.0, 0.0).astype(BF16)
        ranks = dot(jnp.where(mask, 1.0, 0.0).astype(BF16), earlier)
        rank = jnp.sum(jnp.where(mask, ranks, 0.0), axis=0, keepdims=True)
        return route.astype(F32) * float(cap) + rank

    def choose(r, k, target):
        slots = lax.broadcasted_iota(jnp.int32, (cap, rows), 0) + mates[k] * cap
        picks = jnp.where(slots.astype(F32) == target, 1.0, 0.0).astype(BF16)
        table[r, fixed(k), :] = picks
        held = sent if k else got
        held[r, fixed(k), :width] = dot(picks, tok[r]).astype(BF16)
        held[r, fixed(k), width:] = dot(picks, og[r]).astype(BF16)

    def dispatch_copy(r, k):
        return pltpu.make_async_remote_copy(
            src_ref=sent.at[r, fixed(k)],
            dst_ref=got.at[r, fixed(k)],
            send_sem=d_send.at[r, k],
            recv_sem=d_recv.at[r, k],
            device_id=(mates[k], node),
            device_id_type=MESH,
        )

    def return_copy(r, k, part):
        some = pl.ds(k * cap + part * (cap // 2), cap // 2)
        return pltpu.make_async_remote_copy(
            src_ref=back.at[r, some],
            dst_ref=ret.at[r, some],
            send_sem=r_send.at[r, k, part],
            recv_sem=r_recv.at[r, k, part],
            device_id=(mates[k], node),
            device_id_type=MESH,
        )

    def z_copy(r, way, j, held=shared):
        return pltpu.make_async_remote_copy(
            src_ref=held.at[r, bit(j)],
            dst_ref=beside.at[r, way, bit(j)],
            send_sem=z_send.at[r, way, j],
            recv_sem=z_recv.at[r, way, j],
            device_id=(expert, way * down + (1 - way) * up),
            device_id_type=MESH,
        )

    def x_copy(r, j, held=pair):
        return pltpu.make_async_remote_copy(
            src_ref=held.at[r, bit(j)],
            dst_ref=across.at[r, bit(j)],
            send_sem=x_send.at[r, j],
            recv_sem=x_recv.at[r, j],
            device_id=(expert, facing),
            device_id_type=MESH,
        )

    def start_return(r, k):
        for part in range(2):
            return_copy(r, k, part).start()

    def slopes(r, half):
        part = pl.ds(half * rows, rows)
        pre = dot(got[r, part, :width], wide[...]) * factor
        grads = got[r, part, width:].astype(F32)
        slope[part, :] = (grads * 2.0 * jnp.maximum(pre, 0.0)).astype(BF16)

    def update_moment(r):
        total = jnp.zeros((1, hidden), F32)
        for j in range(CHUNKS):
            rung = pl.ds(j * tile, tile)
            grad = dot(got[r, :, rung], slope[...], 0, 0) * factor
            new = 0.9 * moment[rung, :] + grad
            moment[rung, :] = new
            total = total + jnp.sum(new * new, axis=0, keepdims=True)
        norm = jnp.sqrt(jnp.sum(total, axis=1, keepdims=True))
        scale = 1.0 / (norm + 1e-07)
        for j in range(CHUNKS):
            rung = pl.ds(j * tile, tile)
            orthog[rung, :] = (moment[rung, :] * scale).astype(BF16)

    def polynomial():
        part = hidden // 2
        for i in range(2):
            columns = pl.ds(i * part, part)
            gram[columns, :] = dot(orthog[:, columns], orthog[...], 0, 0).astype(BF16)
        for i in range(2):
            columns = pl.ds(i * part, part)
            own = gram[columns, :]
            square = dot(own, gram[...])
            poly[columns, :] = (-4.775 * own.astype(F32) + 2.0315 * square).astype(BF16)

    def applied(j):
        own = orthog[pl.ds(j * tile, tile), :]
        return (3.4445 * own.astype(F32) + dot(own, poly[...])).astype(BF16)

    def orthogonalize_and_share(r):
        def sweep(i, carry):
            polynomial()
            for j in range(CHUNKS):
                orthog[pl.ds(j * tile, tile), :] = applied(j)
            return carry

        lax.fori_loop(0, NS_STEPS - 1, sweep, 0)
        polynomial()
        for j in range(CHUNKS):
            rung = pl.ds(j * tile, tile)
            stepped = weight[rung, :] - step_size * applied(j).astype(F32)
            weight[rung, :] = stepped
            shared[r, rung, :] = stepped.astype(BF16)
            for i in range(j * (PIECES // CHUNKS), (j + 1) * (PIECES // CHUNKS)):
                if i < EARLY:
                    x_copy(r, i, shared).start()
                else:
                    z_copy(r, 0, i).start()
                    z_copy(r, 1, i).start()

    def backward(r, k, blocks):
        part = pl.ds(k * cap, blocks * cap)
        for j in range(CHUNKS):
            rung = pl.ds(j * tile, tile)
            grad = dot(slope[part, :], wide[rung, :], 1, 1) * factor
            back[r, part, rung] = grad.astype(BF16)
        if k == 0:
            ret[r, fixed(0), :] = back[r, fixed(0), :]

    def unsort(r, k, blocks):
        for i in range(max(k, 1), k + blocks):
            return_copy(r, i, 0).wait_recv()
            return_copy(r, i, 1).wait_recv()
        part = pl.ds(k * cap, blocks * cap)

        for j in range(CHUNKS):
            columns = pl.ds(j * tile, tile)
            placed = dot(table[r, part, :], ret[r, part, columns], 0, 0)
            if k:
                placed = placed + ig[r, :, columns].astype(F32)
            ig[r, :, columns] = placed.astype(BF16)

    def pass_across(r, first, last):
        def body(j, carry):
            z_copy(r, 1 - odd, j).wait_recv()
            own = shared[r, bit(j), :].astype(F32)
            pair[r, bit(j), :] = (own + beside[r, 1 - odd, bit(j), :].astype(F32)).astype(BF16)
            x_copy(r, j).start()
            return carry

        lax.fori_loop(first, last, body, 0)

    def pass_along(r):
        for j in range(EARLY):
            z_copy(r, 1 - odd, j).start()
            x_copy(r, j, shared).wait_recv()
            own = shared[r, bit(j), :].astype(F32)
            pair[r, bit(j), :] = (own + across[r, bit(j), :].astype(F32)).astype(BF16)
            z_copy(r, odd, j, pair).start()

    def averaged(r, j):
        neighbours = beside[r, 0, bit(j), :].astype(F32) + beside[r, 1, bit(j), :].astype(F32)
        neighbours = neighbours + across[r, bit(j), :].astype(F32)
        new = 0.4 * weight[bit(j), :] + 0.15 * neighbours
        weight[bit(j), :] = new
        return new

    def averages(r, use):
        for j in range(EARLY):
            z_copy(r, 0, j).wait_recv()
            z_copy(r, 1, j).wait_recv()
            use(j, averaged(r, j))

        def body(j, carry):
            z_copy(r, odd, j).wait_recv()
            x_copy(r, j).wait_recv()
            use(j, averaged(r, j))
            return carry

        lax.fori_loop(EARLY, PIECES, body, 0)

    load_route.wait()
    target = targets(0)
    loads[0].wait()
    loads[1].wait()
    for copy in (loads[2], loads[3], load_w, load_m):
        copy.start()
    choose(0, 2, target)
    pl.semaphore_wait(barrier, 3 + odd + led_up + (1 - led))

    @pl.when(led_up == 1)
    def _():
        pl.semaphore_signal(ready.at[0], inc=1, device_id=(expert, up), device_id_type=MESH)

    @pl.when(led == 0)
    def _():
        pl.semaphore_signal(ready.at[2], inc=1, device_id=(expert, down), device_id_type=MESH)

    @pl.when(odd == 1)
    def _():
        pl.semaphore_signal(ready.at[1], inc=1, device_id=(expert, facing), device_id_type=MESH)

    dispatch_copy(0, 2).start()
    for k in (3, 1):
        choose(0, k, target)
        dispatch_copy(0, k).start()
    choose(0, 0, target)
    target = targets(1)
    loads[2].wait()
    loads[3].wait()
    for k in (2, 3, 1):
        choose(1, k, target)
        dispatch_copy(1, k).start()
    choose(1, 0, target)
    load_w.wait()

    def narrow(j, carry):
        wide[strip(j), :] = weight[strip(j), :].astype(BF16)
        return carry

    lax.fori_loop(0, CHUNKS, narrow, 0)
    load_m.wait()
    dispatch_copy(0, 1).wait_recv()
    slopes(0, 0)
    dispatch_copy(0, 2).wait_recv()
    dispatch_copy(0, 3).wait_recv()
    slopes(0, 1)
    update_moment(0)

    @pl.when(led == 1)
    def _():
        pl.semaphore_wait(ready.at[0], 1)

    @pl.when(led_up == 0)
    def _():
        pl.semaphore_wait(ready.at[2], 1)

    @pl.when(odd == 0)
    def _():
        pl.semaphore_wait(ready.at[1], 1)

    orthogonalize_and_share(0)
    backward(0, 2, 2)
    backward(0, 0, 2)
    pass_across(0, EARLY, PIECES)
    for k in (2, 3, 1):
        start_return(0, k)
    pass_along(0)

    def narrowed(j, new):
        wide[bit(j), :] = new.astype(BF16)

    averages(0, narrowed)

    for k in (1, 2, 3):
        dispatch_copy(1, k).wait_recv()
    slopes(1, 0)
    slopes(1, 1)
    backward(1, 2, 1)
    start_return(1, 2)
    update_moment(1)
    orthogonalize_and_share(1)
    backward(1, 3, 1)
    return_copy(1, 3, 0).start()
    backward(1, 0, 2)
    start_return(1, 1)
    pass_across(1, EARLY, PIECES // 2)
    unsort(0, 0, 4)
    pass_across(1, PIECES // 2, PIECES)
    return_copy(1, 3, 1).start()
    pass_along(1)
    unsort(1, 0, 3)
    averages(1, lambda j, new: None)
    unsort(1, 3, 1)

    for r in range(ROUNDS):
        for k in (1, 2, 3):
            dispatch_copy(r, k).wait_send()
            return_copy(r, k, 0).wait_send()
            return_copy(r, k, 1).wait_send()

        def sent_all(j, carry, r=r):
            z_copy(r, 0, j).wait_send()
            z_copy(r, 1, j).wait_send()
            x_copy(r, j).wait_send()
            return carry

        lax.fori_loop(0, PIECES, sent_all, 0)


def store(weight, moment, ig, w_out, m_out, ig_out, sems):
    copies = (
        pltpu.make_async_copy(weight, w_out.at[0, 0], sems.at[0]),
        pltpu.make_async_copy(moment, m_out.at[0, 0], sems.at[1]),
        pltpu.make_async_copy(ig, ig_out, sems.at[2]),
    )
    for copy in copies:
        copy.start()
    for copy in copies:
        copy.wait()


def on_device(tokens, routing, out_grad, weights, momentum):
    rounds, rows, width = tokens.shape
    hidden = out_grad.shape[2]
    experts = weights.shape[1] * lax.axis_size("expert")
    nodes = lax.axis_size("node")
    slots = experts * (rows // 2)
    anywhere = pl.BlockSpec(memory_space=pl.ANY)
    in_hbm = pl.BlockSpec(memory_space=pltpu.HBM)
    on_chip = pl.BlockSpec(memory_space=pltpu.VMEM)
    dma = pltpu.SemaphoreType.DMA
    operands = (
        pltpu.with_memory_space_constraint(x, pltpu.HBM)
        for x in (tokens, routing, out_grad, weights, momentum)
    )
    weight, moment, in_grad = pl.pallas_call(
        functools.partial(kernel, nodes),
        name="muon_rounds",
        out_shape=(
            pltpu.VMEM((width, hidden), F32),
            pltpu.VMEM((width, hidden), F32),
            pltpu.VMEM((rounds, rows, width), BF16),
        ),
        in_specs=[in_hbm] * 5,
        out_specs=(on_chip, on_chip, on_chip),
        scratch_shapes=[
            pltpu.VMEM((rounds, rows), jnp.int32),
            pltpu.VMEM((rounds, rows, width), BF16),
            pltpu.VMEM((rounds, rows, hidden), BF16),
            pltpu.VMEM((width, hidden), BF16),
            pltpu.VMEM((rounds, slots, rows), BF16),
            pltpu.VMEM((rounds, slots, width + hidden), BF16),
            pltpu.VMEM((rounds, slots, width + hidden), BF16),
            pltpu.VMEM((slots, hidden), BF16),
            pltpu.VMEM((width, hidden), BF16),
            pltpu.VMEM((hidden, hidden), BF16),
            pltpu.VMEM((hidden, hidden), BF16),
            pltpu.VMEM((rounds, slots, width), BF16),
            pltpu.VMEM((rounds, slots, width), BF16),
            pltpu.VMEM((rounds, width, hidden), BF16),
            pltpu.VMEM((rounds, 2, width, hidden), BF16),
            pltpu.VMEM((rounds, width, hidden), BF16),
            pltpu.VMEM((rounds, width, hidden), BF16),
            dma((7,)),
            dma((rounds, 4)),
            dma((rounds, 4)),
            dma((rounds, 4, 2)),
            dma((rounds, 4, 2)),
            dma((rounds, 2, PIECES)),
            dma((rounds, 2, PIECES)),
            dma((rounds, PIECES)),
            dma((rounds, PIECES)),
            pltpu.SemaphoreType.REGULAR((3,)),
        ],
        compiler_params=pltpu.CompilerParams(
            collective_id=0, has_side_effects=True, vmem_limit_bytes=40 << 20
        ),
    )(*operands)
    return pl.pallas_call(
        store,
        name="store_results",
        out_shape=(
            jax.ShapeDtypeStruct(weights.shape, F32),
            jax.ShapeDtypeStruct(momentum.shape, F32),
            jax.ShapeDtypeStruct(tokens.shape, BF16),
        ),
        in_specs=[anywhere, anywhere, anywhere],
        out_specs=(anywhere, anywhere, anywhere),
        scratch_shapes=[dma((3,))],
        compiler_params=pltpu.CompilerParams(vmem_limit_bytes=1 << 20),
    )(weight, moment, in_grad)


def solution(mesh):
    return jax.shard_map(
        on_device,
        mesh=mesh,
        in_specs=(
            P(None, ("expert", "node"), None),
            P(None, ("expert", "node")),
            P(None, ("expert", "node"), None),
            P("node", "expert", None, None),
            P("node", "expert", None, None),
        ),
        out_specs=(
            P("node", "expert", None, None),
            P("node", "expert", None, None),
            P(None, ("expert", "node"), None),
        ),
        check_vma=False,
    )
```
